128 devices in a mesh: axial: 8 (over x, core), azim: 16 (over z, y).
Axes of the slice: x: 4, y: 4, z: 4, core: 2. Of those that a mesh axis runs over, the one named last changes fastest.
Arguments:
- cycle_state: float32 [5, 64, 2048, 256], P(None, 'axial', 'azim'), as said below
- core_state: float32 [5, 64, 192, 192], P(None, 'axial', 'azim'), as said below
- core_taps: int32 [768, 4], replicated, may hold values from 0 to 2047, as said below
- core_weights: float32 [768, 4], replicated, may hold values from 0.1 to 1
- cycle_taps: int32 [2048, 4], replicated, may hold values from 0 to 36863, as said below
- cycle_weights: float32 [2048, 4], replicated, may hold values from 0.1 to 1
Outputs:
- cycle_new: float32 [5, 64, 2048, 256], P(None, 'axial', 'azim')
- core_new: float32 [5, 64, 192, 192], P(None, 'axial', 'azim')
The draws below stay inside these ranges and needn't reach their ends.
Inputs may be any that keep to these rules, and one draw needn't show every extreme that they name: `core_taps`: cycle positions, each within 8 positions (cyclically) of position g * 2048 // 768. `cycle_taps`: flat indices of core cells within three cells of the core's edge. `cycle_state`: density (component 0) lies in 0.5 to 1.5. `core_state`: density (component 0) lies in 0.5 to 1.5.
All inputs are finite; a program needn't handle non-finite values.
Results may differ from the reference program's by a relative error of at most 0.0003.
Values sent between devices are 32-bit elements; how exact they have to be, the bound alone decides.
A program may use at most 128 MiB of HBM per device.

```python
import math
import jax
import jax.numpy as jnp
from jax import lax

CA = 8
R = 256
CORE_N = 192
TAPS = 4
NX = 64
NT = 2048
GHOST = 768


def state_law(key, shape):
    keys = jax.random.split(key, 3)
    density = jax.random.uniform(keys[0], shape, jnp.float32, 0.5, 1.5)
    momenta = 0.6 * jax.random.normal(keys[1], (3,) + shape, jnp.float32)
    momenta = jnp.clip(momenta, -3.0, 3.0)
    energy = jax.random.uniform(keys[2], shape, jnp.float32, 2.0, 4.0)
    return jnp.concatenate([density[None], momenta, energy[None]], axis=0)


def draw_cycle_state(key, part):
    return state_law(jax.random.fold_in(key, 11), (NX, NT, R))


def draw_core_state(key, part):
    return state_law(jax.random.fold_in(key, 13), (NX, CORE_N, CORE_N))


def draw_core_taps(key, part):
    base = jnp.arange(GHOST, dtype=jnp.int32) * NT // GHOST
    jitter = jax.random.randint(jax.random.fold_in(key, 17), (GHOST, TAPS), -8, 9)
    taps = ((base[:, None] + jitter) % NT).astype(jnp.int32)
    taps = taps.at[0, 0].set(NT - 1)
    taps = taps.at[0, 1].set(0)
    return taps.astype(jnp.int32)


def draw_cycle_taps(key, part):
    perimeter = jnp.arange(NT, dtype=jnp.int32) * GHOST // NT
    jitter = jax.random.randint(jax.random.fold_in(key, 19), (NT, TAPS), -4, 5)
    inward = jax.random.randint(jax.random.fold_in(key, 23), (NT, TAPS), 0, 3)
    spot = (perimeter[:, None] + jitter) % GHOST
    side = spot // CORE_N
    along = spot % CORE_N
    row_idx = jnp.where(side < 2, along, jnp.where(side == 2, inward, CORE_N - 1 - inward))
    col_idx = jnp.where(side == 0, inward, jnp.where(side == 1, CORE_N - 1 - inward, along))
    taps = (row_idx * CORE_N + col_idx).astype(jnp.int32)
    taps = taps.at[0, 0].set(0)
    taps = taps.at[NT // 2 - 1, 0].set(CORE_N * CORE_N - 1)
    return taps.astype(jnp.int32)


def setup_inputs(seed: int = 0) -> dict:
    key_list = jax.random.split(jax.random.key(seed), 7)
    cycle_state = draw_cycle_state(jax.random.fold_in(key_list[6], 71), 0)
    core_state = draw_core_state(jax.random.fold_in(key_list[6], 71), 0)
    core_taps = draw_core_taps(jax.random.fold_in(key_list[6], 71), 0)
    core_weights = jnp.clip(jax.random.uniform(key_list[3], (GHOST, TAPS), jnp.float32, 0.1, 1.0), 0.1, 1.0)
    cycle_taps = draw_cycle_taps(jax.random.fold_in(key_list[6], 71), 0)
    cycle_weights = jnp.clip(jax.random.uniform(key_list[5], (NT, TAPS), jnp.float32, 0.1, 1.0), 0.1, 1.0)
    return dict(cycle_state=cycle_state, core_state=core_state, core_taps=core_taps, core_weights=core_weights, cycle_taps=cycle_taps, cycle_weights=cycle_weights)


time_step = 0.001
axial_step = 0.004
radial_step = 1.0 / 256.0
core_step = 2.0 / 192.0
inner_radius = 1.0
viscosity = 0.002
gamma_minus = 0.4


def pressure_of(state):
    kinetic = 0.5 * (state[1] * state[1] + state[2] * state[2] + state[3] * state[3]) / state[0]
    return gamma_minus * (state[4] - kinetic)


def fluxes(state, component):
    pressure = pressure_of(state)
    velocity = state[component] / state[0]
    parts = [state[component], state[1] * velocity, state[2] * velocity, state[3] * velocity, (state[4] + pressure) * velocity]
    parts[component] = parts[component] + pressure
    return jnp.stack(parts, axis=0)


def angle_of(positions, total):
    return (positions.astype(jnp.float32) + 0.5) * (2.0 * math.pi / total)


def to_cartesian(trace, angles):
    cosine = jnp.cos(angles)
    sine = jnp.sin(angles)
    y_part = trace[3] * cosine - trace[2] * sine
    z_part = trace[3] * sine + trace[2] * cosine
    return jnp.stack([trace[0], trace[1], y_part, z_part, trace[4]], axis=0)


def to_polar(trace, angles):
    cosine = jnp.cos(angles)
    sine = jnp.sin(angles)
    azimuthal = trace[3] * cosine - trace[2] * sine
    radial = trace[2] * cosine + trace[3] * sine
    return jnp.stack([trace[0], trace[1], azimuthal, radial, trace[4]], axis=0)


def interpolate(values, taps, weights):
    normed = weights / jnp.sum(weights, axis=1, keepdims=True)
    picked = jnp.take(values, taps, axis=2)
    return jnp.sum(picked * normed, axis=3)


def radius_full(count):
    return inner_radius + (jnp.arange(count + 2).astype(jnp.float32) - 0.5) * radial_step


def cycle_rhs(padded, inner_ghost, angle_step):
    center = padded[:, 1:-1, 1:-1]
    reflect = jnp.array([1.0, 1.0, 1.0, -1.0, 1.0], jnp.float32)[:, None, None]
    outer_ghost = center[:, :, :, -1] * reflect
    radial_pad = jnp.concatenate([inner_ghost[..., None], center, outer_ghost[..., None]], axis=3)
    radius = radius_full(center.shape[3])
    mid_radius = radius[1:-1]
    arc = angle_step * mid_radius
    axial_flux = fluxes(padded[:, :, 1:-1], 1)
    azim_flux = fluxes(padded[:, 1:-1], 2)
    radial_flux = fluxes(radial_pad, 3)
    divergence = (axial_flux[:, 2:] - axial_flux[:, :-2]) / (2.0 * axial_step)
    divergence = divergence + (azim_flux[:, :, 2:] - azim_flux[:, :, :-2]) / (2.0 * arc)
    divergence = divergence + (radius[2:] * radial_flux[..., 2:] - radius[:-2] * radial_flux[..., :-2]) / (2.0 * radial_step * mid_radius)
    laplace = (padded[:, 2:, 1:-1] - 2.0 * center + padded[:, :-2, 1:-1]) / (axial_step * axial_step)
    laplace = laplace + (padded[:, 1:-1, 2:] - 2.0 * center + padded[:, 1:-1, :-2]) / (arc * arc)
    laplace = laplace + (radial_pad[..., 2:] - 2.0 * center + radial_pad[..., :-2]) / (radial_step * radial_step)
    pressure = pressure_of(center)
    swirl = -center[2] * center[3] / (center[0] * mid_radius)
    outward = (center[2] * center[2] / center[0] + pressure) / mid_radius
    zero_part = jnp.zeros_like(swirl)
    source = jnp.stack([zero_part, zero_part, swirl, outward, zero_part], axis=0)
    return -divergence + source + viscosity * laplace


def core_rhs(axial_pad, row_pad, left_col, right_col):
    center = axial_pad[:, 1:-1]
    col_pad = jnp.concatenate([left_col[..., None], center, right_col[..., None]], axis=3)
    axial_flux = fluxes(axial_pad, 1)
    row_flux = fluxes(row_pad, 2)
    col_flux = fluxes(col_pad, 3)
    divergence = (axial_flux[:, 2:] - axial_flux[:, :-2]) / (2.0 * axial_step)
    divergence = divergence + (row_flux[:, :, 2:] - row_flux[:, :, :-2]) / (2.0 * core_step)
    divergence = divergence + (col_flux[..., 2:] - col_flux[..., :-2]) / (2.0 * core_step)
    laplace = (axial_pad[:, 2:] - 2.0 * center + axial_pad[:, :-2]) / (axial_step * axial_step)
    laplace = laplace + (row_pad[:, :, 2:] - 2.0 * center + row_pad[:, :, :-2]) / (core_step * core_step)
    laplace = laplace + (col_pad[..., 2:] - 2.0 * center + col_pad[..., :-2]) / (core_step * core_step)
    return -divergence + viscosity * laplace


def reference(cycle_state, core_state, core_taps, core_weights, cycle_taps, cycle_weights):
    channels, planes, positions_all, radial_cells = cycle_state.shape
    core_cells = core_state.shape[3]
    angles = angle_of(jnp.arange(positions_all), positions_all)
    angle_step = 2.0 * math.pi / positions_all
    cart_trace = to_cartesian(cycle_state[:, :, :, 0], angles)
    ghosts = interpolate(cart_trace, core_taps, core_weights)
    axial_pad = jnp.concatenate([core_state[:, -1:], core_state, core_state[:, :1]], axis=1)
    lower = ghosts[:, :, 2 * core_cells:3 * core_cells]
    upper = ghosts[:, :, 3 * core_cells:4 * core_cells]
    row_pad = jnp.concatenate([lower[:, :, None], core_state, upper[:, :, None]], axis=2)
    left_col = ghosts[:, :, 0:core_cells]
    right_col = ghosts[:, :, core_cells:2 * core_cells]
    core_new = core_state + time_step * core_rhs(axial_pad, row_pad, left_col, right_col)
    flat_core = core_state.reshape(channels, planes, core_cells * core_cells)
    inner_ghost = to_polar(interpolate(flat_core, cycle_taps, cycle_weights), angles)
    count = planes // CA

    def one_block(block):
        index_list = ((block * CA - 1 + jnp.arange(CA + 2)) % planes).astype(jnp.int32)
        slab = jnp.take(cycle_state, index_list, axis=1)
        slab = jnp.concatenate([slab[:, :, -1:], slab, slab[:, :, :1]], axis=2)
        inner_part = lax.dynamic_slice_in_dim(inner_ghost, (block * CA).astype(jnp.int32), CA, 1)
        own_part = lax.dynamic_slice_in_dim(cycle_state, (block * CA).astype(jnp.int32), CA, 1)
        return own_part + time_step * cycle_rhs(slab, inner_part, angle_step)

    stacked = lax.map(one_block, jnp.arange(count).astype(jnp.int32))
    cycle_new = jnp.moveaxis(stacked, 0, 1).reshape(channels, planes, positions_all, radial_cells)
    return cycle_new, core_new
```

```python
import functools
import math

import jax
import jax.numpy as jnp
import numpy as np
from jax import lax
from jax.experimental import pallas as pl
from jax.experimental.pallas import tpu as pltpu
from jax.sharding import PartitionSpec as P

DT = 0.001
DX = 0.004
DR = 1.0 / 256.0
DC = 2.0 / 192.0
NU = 0.002
NT = 2048
NR = 256
NC = 192
PL = 8
SEC = 128
ROWS = 12
NA = 16
DA = 2.0 * math.pi / NT

BX = NU * DT / DX**2
AX = DT / (2.0 * DX)
BR = NU * DT / DR**2 / BX
AC = DT / (2.0 * DC) / BX
BC = NU * DT / DC**2 / BX
SX = DX / (2.0 * NU)


def tables():
    radius = lambda i: 1.0 + (i + 0.5) / 256.0
    i = np.arange(NR, dtype=np.float64)
    tab = np.zeros((8, NR))
    tab[0] = DT / (2.0 * DA * radius(i)) / BX
    tab[1] = NU * DT / (DA * radius(i)) ** 2 / BX
    tab[2] = DT * radius(i) / (2.0 * DR * radius(i - 1)) / BX
    tab[3] = DT * radius(i) / (2.0 * DR * radius(i + 1)) / BX
    tab[3, -1] = DT * radius(NR) / (2.0 * DR * radius(NR - 1)) / BX
    tab[4] = 1.0 / BX - 2.0 - 2.0 * BR - 2.0 * tab[1]
    tab[5] = DT / radius(i) / BX
    angle = (np.arange(NT) + 0.5) * (2.0 * math.pi / NT)
    trig = np.zeros((8, NT))
    trig[0] = np.cos(angle)
    trig[1] = np.sin(angle)
    return tab.astype(np.float32), trig.astype(np.float32)


INNER = float(DT * (1.0 - 0.5 / 256.0) / (2.0 * DR * (1.0 + 0.5 / 256.0)) / BX)
CC = float(1.0 / BX - 2.0 - 4.0 * BC)


def needed(a):
    found = set()
    for off in (0, 512):
        found |= {((32 * a - 8 + off) // SEC) % NA, ((32 * a + 37 + off) // SEC) % NA}
    if a == 0:
        found |= set(range(7, 13))
    if a == NA - 1:
        found |= {11, 12, 13, 14, 15, 0}
    return sorted(found)


def point(q):
    inv = pl.reciprocal(q[0], approx=False)
    u1, u2, u3 = q[1] * inv, q[2] * inv, q[3] * inv
    p11, p22, p33 = q[1] * u1, q[2] * u2, q[3] * u3
    pr = 0.4 * q[4] - 0.2 * (p11 + p22 + p33)
    return (u1, u2, u3), (p11, p22, p33), pr, q[4] + pr


def flux(q, pt, k):
    u, sq, pr, h = pt
    v = u[k - 1]
    out = [q[k], q[1] * v, q[2] * v, q[3] * v, h * v]
    out[k] = sq[k - 1] + pr
    return out


def kernel(
    cyc, cor, ctaps, cwts, ytaps, ywts, tab_in, trig_in, cyc_out, cor_out,
    qv, ov, p2s, m2s, ah, cin, cv, oc, chx, crlo, crhi, cres, trs, trr, shs, shr, xm,
    gl, gr, tab, trig, ct, cw, yt, yw,
    in_sem, sm_sem, out_sem, ax_s, ax_r, cx_s, cx_r, ar_s, ar_r, cr_s, cr_r, tr_s, tr_r, sh_s, sh_r,
):
    me = lax.axis_index("azim")
    ax = lax.axis_index("axial")
    n_ax = lax.axis_size("axial")
    up_ax = {"axial": lax.rem(ax + 1, n_ax)}
    dn_ax = {"axial": lax.rem(ax + n_ax - 1, n_ax)}
    up_az = {"azim": lax.rem(me + 1, NA)}
    dn_az = {"azim": lax.rem(me + NA - 1, NA)}
    MESH = pl.DeviceIdType.MESH

    barrier = pltpu.get_barrier_semaphore()
    pl.semaphore_signal(barrier, inc=1, device_id=up_ax, device_id_type=MESH)
    pl.semaphore_signal(barrier, inc=1, device_id=dn_ax, device_id_type=MESH)

    def greet(d, _):
        @pl.when(d != me)
        def _():
            pl.semaphore_signal(barrier, inc=1, device_id={"azim": d}, device_id_type=MESH)

        return 0

    lax.fori_loop(0, NA, greet, 0)

    smalls = [
        pltpu.make_async_copy(s, d, sm_sem.at[i])
        for i, (s, d) in enumerate(
            [(cor, cin), (ytaps, yt), (ywts, yw), (tab_in, tab), (trig_in, trig), (ctaps, ct), (cwts, cw)]
        )
    ]
    planes = [pltpu.make_async_copy(cyc.at[:, p], qv.at[:, p + 1], in_sem.at[p]) for p in range(PL)]
    for c in smalls:
        c.start()
    for c in planes:
        c.start()

    def remote(src, dst, s, r, dev):
        return pltpu.make_async_remote_copy(
            src_ref=src, dst_ref=dst, send_sem=s, recv_sem=r, device_id=dev, device_id_type=MESH
        )

    axial = [
        remote(cyc.at[:, 0], qv.at[:, PL + 1], ax_s.at[0], ax_r.at[0], dn_ax),
        remote(cyc.at[:, PL - 1], qv.at[:, 0], ax_s.at[1], ax_r.at[1], up_ax),
    ]
    caxial = [
        remote(cor.at[:, :, 0, :], chx.at[:, :, PL - 1, :], cx_s.at[0], cx_r.at[0], dn_ax),
        remote(cor.at[:, :, PL - 1, :], chx.at[:, :, 0, :], cx_s.at[1], cx_r.at[1], up_ax),
    ]
    azim = [
        remote(cyc.at[:, :, 0, :], ah.at[:, :, 7, :], ar_s.at[0], ar_r.at[0], dn_az),
        remote(cyc.at[:, :, SEC - 1, :], ah.at[:, :, 0, :], ar_s.at[1], ar_r.at[1], up_az),
    ]
    crow_dn = remote(cor.at[:, 0], crhi, cr_s.at[0], cr_r.at[0], dn_az)
    crow_up = remote(cor.at[:, ROWS - 1], crlo, cr_s.at[1], cr_r.at[1], up_az)

    lane8 = lax.broadcasted_iota(jnp.int32, (8, 128), 1)
    row8 = lax.broadcasted_iota(jnp.int32, (8, 128), 0)

    pl.semaphore_wait(barrier, NA - 1 + 2)
    for c in axial:
        c.start()
    for c in azim + caxial:
        c.start()

    @pl.when(me > 0)
    def _():
        crow_dn.start()

    @pl.when(me < NA - 1)
    def _():
        crow_up.start()

    for c in smalls:
        c.wait()

    def pad(i, _):
        for c in range(5):
            cv[c, i + 1, :, 0:128] = cin[c, i, :, 0:128]
            cv[c, i + 1, :, 128:192] = cin[c, i, :, 128:192]
        return 0

    lax.fori_loop(0, ROWS, pad, 0)

    for c in planes:
        c.wait()

    lane_s = lax.broadcasted_iota(jnp.int32, (SEC, 128), 1)

    def trace(p, t):
        for c in range(5):
            ch = c * 8 + p
            t = jnp.where(lane_s == ch, pltpu.roll(qv[c, p + 1, :, 0:128], ch, 1), t)
        return t

    tt = lax.fori_loop(0, PL, trace, jnp.zeros((SEC, 128), jnp.float32)).T
    own = pl.ds(pl.multiple_of(me * SEC, SEC), SEC)
    cosine = jnp.broadcast_to(trig[0:1, own], (8, 128))
    sine = jnp.broadcast_to(trig[1:2, own], (8, 128))
    tq = [tt[8 * c : 8 * c + 8, :] for c in range(5)]
    cart = [tq[0], tq[1], tq[3] * cosine - tq[2] * sine, tq[3] * sine + tq[2] * cosine, tq[4]]
    for c in range(5):
        trs[c] = cart[c]
        trr[me, c] = cart[c]

    def tr_copy(d):
        return remote(trs, trr.at[me], tr_s.at[d], tr_r.at[me], {"azim": d})

    def is_in(x, items):
        hit = x == items[0]
        for it in items[1:]:
            hit = jnp.logical_or(hit, x == it)
        return hit

    for a in range(NA):
        others = [s for s in needed(a) if s != a]

        @pl.when(is_in(me, others))
        def _(a=a):
            tr_copy(a).start()

    vcol = []
    for c in range(5):
        v = jnp.zeros((8, 128), jnp.float32)
        for i in range(ROWS):
            left = pltpu.roll(cv[c, i + 1, :, 0:128], 8 * i, 1)
            right = pltpu.roll(cv[c, i + 1, :, 128:256], (8 * i + 4 - 60) % 128, 1)
            v = jnp.where((lane8 >> 3) == i, jnp.where((lane8 & 7) < 4, left, right), v)
        vcol.append(v)
    for c in range(5):
        xm[c * 8 : c * 8 + 8, :] = vcol[c]

    def bcast(x):
        return jnp.broadcast_to(x, (8, 128))

    edge = jnp.logical_or(me == 0, me == NA - 1)
    r0 = jnp.where(me == 0, 0, ROWS - 4)

    def share(d, _):
        cols = pl.ds(pl.multiple_of(d * SEC, SEC), SEC)
        ws = [yw[k : k + 1, cols] for k in range(4)]
        total = ws[0] + ws[1] + ws[2] + ws[3]
        acc = [jnp.zeros((8, 128), jnp.float32) for _ in range(5)]
        for k in range(4):
            tap = bcast(yt[k : k + 1, cols])
            w = bcast(ws[k] / total)
            row = ((tap >> 6) * 43691) >> 17
            col = tap - row * NC
            lrow = row - me * ROWS
            inside = jnp.logical_and(lrow >= 0, lrow < ROWS)
            side = jnp.logical_or(col < 4, col >= NC - 4)
            ok = jnp.logical_and(inside, side)
            idx = (lrow * 8 + jnp.where(col < 4, col, col - (NC - 8))) & 127
            wk = jnp.where(ok, w, 0.0)
            for c in range(5):
                got = jnp.take_along_axis(xm[c * 8 : c * 8 + 8, :], idx, axis=1)
                acc[c] = acc[c] + wk * got
        for c in range(5):
            shs[d, c] = acc[c]

        @pl.when(edge)
        def _():
            extra = [jnp.zeros((8, 128), jnp.float32) for _ in range(5)]
            for k in range(4):
                tap = bcast(yt[k : k + 1, cols])
                w = bcast(ws[k] / total)
                row = ((tap >> 6) * 43691) >> 17
                col = tap - row * NC
                erow = row - me * ROWS - r0
                mid = jnp.logical_and(col >= 4, col < NC - 4)
                idx = col & 127
                high = col >= 128
                for r in range(4):
                    wk = jnp.where(jnp.logical_and(mid, erow == r), w, 0.0)
                    for c in range(5):
                        lo = jnp.take_along_axis(cv[c, r0 + r + 1, :, 0:128], idx, axis=1)
                        hi = jnp.take_along_axis(cv[c, r0 + r + 1, :, 128:256], idx, axis=1)
                        extra[c] = extra[c] + wk * jnp.where(high, hi, lo)
            for c in range(5):
                shs[d, c] += extra[c]

        @pl.when(d != me)
        def _():
            sh_copy(d).start()

        @pl.when(d == me)
        def _():
            for c in range(5):
                shr[d, c] = shs[d, c]

        return 0

    def sh_copy(d):
        return remote(shs.at[d], shr.at[me], sh_s.at[d], sh_r.at[me], {"azim": d})

    lax.fori_loop(0, NA, share, 0)

    lane = lax.broadcasted_iota(jnp.int32, (8, 128), 1)
    first, last = lane == 0, lane == 127

    zero8 = jnp.zeros((8, 128), jnp.float32)
    for c in range(5):
        for h in range(2):
            m2s[c, h, 8:16, :] = zero8
            p2s[c, h, 144:152, :] = zero8

    def clear(b, _):
        rows = pl.ds(pl.multiple_of(b * 8, 8), 8)
        for c in range(5):
            ov[c, 1, rows, :] = jnp.zeros((8, NR), jnp.float32)
        return 0

    lax.fori_loop(1, 17, clear, 0)

    def finish(p, b):
        rows = pl.ds(pl.multiple_of((b + 1) * 8, 8), 8)
        for c in range(5):
            for h in range(2):
                half = slice(128 * h, 128 * h + 128)
                up = p2s[c, h, pl.ds(b * 8 + 17, 8), :]
                dn = m2s[c, h, pl.ds(b * 8 + 15, 8), :]
                ov[c, p + 1, rows, half] += up + dn

    def cycle_plane(p, _):
        def block(b, _):
            src = pl.ds(pl.multiple_of(b * 8, 8), 8)
            rows = pl.ds(pl.multiple_of((b + 1) * 8, 8), 8)
            srows = pl.ds(pl.multiple_of((b + 2) * 8, 8), 8)
            q = [qv[c, p + 1, src, :] for c in range(5)]
            pt = point(q)
            f1, f2, f3 = flux(q, pt, 1), flux(q, pt, 2), flux(q, pt, 3)
            row = lambda k: jnp.broadcast_to(tab[k : k + 1, :], (8, NR))
            ka, ba, cp, cm, cc, so = [row(k) for k in range(6)]
            for c in range(5):
                m1 = q[c] + f1[c]
                p1 = q[c] - f1[c]
                ov[c, p, rows, :] = BX * (ov[c, p, rows, :] + p1)
                acc = ov[c, p + 1, rows, :] + cc * q[c]
                ov[c, p + 2, rows, :] = m1
                base = BR * q[c]
                p3 = base - cp * f3[c]
                m3 = base + cm * f3[c]
                a, bb = pltpu.roll(p3[:, :128], 127, 1), pltpu.roll(p3[:, 128:], 127, 1)
                wall = m3[:, 128:] if c != 3 else -m3[:, 128:]
                e, f = pltpu.roll(m3[:, :128], 1, 1), pltpu.roll(m3[:, 128:], 1, 1)
                lo = jnp.where(last, bb, a) + jnp.where(first, 0.0, e)
                hi = jnp.where(last, wall, bb) + jnp.where(first, e, f)
                acc = acc + jnp.concatenate([lo, hi], axis=1)
                if c == 2:
                    acc = acc - so * f2[3]
                if c == 3:
                    acc = acc + so * f2[2]
                ov[c, p + 1, rows, :] = acc
                bq = ba * q[c]
                kf = ka * f2[c]
                p2, m2 = bq - kf, bq + kf
                for h in range(2):
                    half = slice(128 * h, 128 * h + 128)
                    p2s[c, h, srows, :] = p2[:, half]
                    m2s[c, h, srows, :] = m2[:, half]
            finish(p, b - 1)
            return 0

        lax.fori_loop(0, SEC // 8, block, 0)
        for c in range(5):
            for h in range(2):
                p2s[c, h, 144:152, :] = zero8
        finish(p, SEC // 8 - 1)
        return 0

    lax.fori_loop(0, PL, cycle_plane, 0)

    for s in range(NA):
        takers = [a for a in range(NA) if s in needed(a) and a != s]

        @pl.when(is_in(me, takers))
        def _(s=s):
            remote(trs, trr.at[s], tr_s.at[s], tr_r.at[s], {"azim": s}).wait_recv()

    s0 = ((32 * me + 2040) >> 7) & 15
    s1 = ((32 * me + 37) >> 7) & 15

    def ghost(start, shift, sectors):
        vals = [zero8 for _ in range(5)]
        ws = [bcast_roll(cw[k : k + 1, start : start + 256], shift) for k in range(4)]
        total = ws[0] + ws[1] + ws[2] + ws[3]
        for k in range(4):
            tap = bcast_roll(ct[k : k + 1, start : start + 256], shift)
            idx = tap & 127
            sec = tap >> 7
            w = ws[k] / total
            for c in range(5):
                v = jnp.take_along_axis(trr[sectors[0], c], idx, axis=1)
                for s in sectors[1:]:
                    v = jnp.where(sec == s, jnp.take_along_axis(trr[s, c], idx, axis=1), v)
                vals[c] = vals[c] + w * v
        return vals

    def bcast_roll(x, shift):
        full = jnp.broadcast_to(x, (8, 256))
        if isinstance(shift, int):
            return full[:, shift : shift + 128]
        return pltpu.roll(full, shift, 1)[:, :128]

    def col_terms(g):
        pt = point(g)
        return flux(g, pt, 3)

    back = lax.rem(512 - ROWS * me, 256)
    g = ghost(0, back, [s0, s1])
    f = col_terms(g)
    for c in range(5):
        gl[c] = BC * g[c] + AC * f[c]
    back = lax.rem(512 - 64 - ROWS * me, 256)
    g = ghost(128, back, [(s0 + 4) & 15, (s1 + 4) & 15])
    f = col_terms(g)
    for c in range(5):
        gr[c] = BC * g[c] - AC * f[c]

    @pl.when(me > 0)
    def _():
        crow_up.wait_recv()
        for c in range(5):
            cv[c, 0, :, 0:128] = crlo[c, :, 0:128]
            cv[c, 0, :, 128:192] = crlo[c, :, 128:192]

    @pl.when(me < NA - 1)
    def _():
        crow_dn.wait_recv()
        for c in range(5):
            cv[c, ROWS + 1, :, 0:128] = crhi[c, :, 0:128]
            cv[c, ROWS + 1, :, 128:192] = crhi[c, :, 128:192]

    @pl.when(me == 0)
    def _():
        for h in range(2):
            g = ghost(384, 0, list(range(7, 13))) if h == 0 else ghost(384, 128, list(range(7, 13)))
            for c in range(5):
                cv[c, 0, :, 128 * h : 128 * h + 128] = g[c]

    @pl.when(me == NA - 1)
    def _():
        g = ghost(512, 64, [11, 12, 13, 14, 15, 0])
        for c in range(5):
            cv[c, ROWS + 1, :, 0:128] = g[c]
        g = ghost(512, 128, [11, 12, 13, 14, 15, 0])
        for c in range(5):
            cv[c, ROWS + 1, :, 128:256] = pltpu.roll(g[c], 64, 1)

    for c in caxial:
        c.wait_recv()

    for c in range(5):
        oc[c, 1] = jnp.zeros((8, 256), jnp.float32)

    def core_row(i, _):
        q = [cv[c, i, :, :] for c in range(5)]
        pt = point(q)
        f1, f2, f3 = flux(q, pt, 1), flux(q, pt, 2), flux(q, pt, 3)
        for h in range(2):
            half = slice(128 * h, 128 * h + (128 if h == 0 else 64))
        x = [chx[c, i - 1, :, :] for c in range(5)]
        x = [jnp.concatenate([v, jnp.ones((8, 64), jnp.float32)], axis=1) for v in x]
        xf = flux(x, point(x), 1)
        sub = lax.broadcasted_iota(jnp.int32, (8, 256), 0)
        for c in range(5):
            m1 = pltpu.roll(q[c] + f1[c], 1, 0)
            p1 = pltpu.roll(q[c] - f1[c], 7, 0)
            m1 = jnp.where(sub == 0, x[c] + xf[c], m1)
            p1 = jnp.where(sub == 7, x[c] - xf[c], p1)
            acc = oc[c, i] + CC * q[c] + m1 + p1
            base = BC * q[c]
            p3, m3 = base - AC * f3[c], base + AC * f3[c]
            a, bb = pltpu.roll(p3[:, :128], 127, 1), pltpu.roll(p3[:, 128:], 127, 1)
            e, f = pltpu.roll(m3[:, :128], 1, 1), pltpu.roll(m3[:, 128:], 1, 1)
            lg = pltpu.roll(gl[c], lax.rem(129 - i, 128), 1)
            rg = pltpu.roll(gr[c], lax.rem(64 + 128 - i, 128), 1)
            lo = jnp.where(last, bb, a) + jnp.where(first, lg, e)
            hi = jnp.where(lane == 63, rg, bb) + jnp.where(first, e, f)
            acc = acc + jnp.concatenate([lo, hi], axis=1)
            p2, m2 = base - AC * f2[c], base + AC * f2[c]
            oc[c, i - 1] = BX * (oc[c, i - 1] + p2)
            oc[c, i] = acc
            oc[c, i + 1] = m2
        return 0

    q = [cv[c, 0, :, :] for c in range(5)]
    f2 = flux(q, point(q), 2)
    for c in range(5):
        oc[c, 1] = BC * q[c] + AC * f2[c]
    lax.fori_loop(1, ROWS + 1, core_row, 0)
    q = [cv[c, ROWS + 1, :, :] for c in range(5)]
    f2 = flux(q, point(q), 2)
    for c in range(5):
        oc[c, ROWS] = BX * (oc[c, ROWS] + BC * q[c] - AC * f2[c])

    def unpad(i, _):
        for c in range(5):
            cres[c, i, :, 0:128] = oc[c, i + 1, :, 0:128]
            cres[c, i, :, 128:192] = oc[c, i + 1, :, 128:192]
        return 0

    lax.fori_loop(0, ROWS, unpad, 0)
    core_done = pltpu.make_async_copy(cres, cor_out, out_sem.at[PL])
    core_done.start()

    def await_share(d, _):
        @pl.when(d != me)
        def _():
            remote(shs.at[d], shr.at[d], sh_s.at[d], sh_r.at[d], {"azim": d}).wait_recv()

        return 0

    lax.fori_loop(0, NA, await_share, 0)
    cart = [functools.reduce(jnp.add, [shr[d, c] for d in range(NA)]) for c in range(5)]
    g = [cart[0], cart[1], cart[3] * cosine - cart[2] * sine, cart[2] * cosine + cart[3] * sine, cart[4]]
    f3 = flux(g, point(g), 3)
    for c in range(5):
        xm[8 * c : 8 * c + 8, :] = BR * g[c] + INNER * f3[c]
    fix = xm[...].T
    for c in azim:
        c.wait_recv()

    def patch(p, _):
        scale = jnp.where(p == PL - 1, 1.0, BX).astype(jnp.float32)
        for c in range(5):
            col = pltpu.roll(fix, lax.rem(128 - (8 * c + p), 128), 1)
            ov[c, p + 1, 8 : 8 + SEC, 0:128] += jnp.where(lane_s == 0, col * scale, 0.0)
        q = [ah[c, p, :, :] for c in range(5)]
        f2 = flux(q, point(q), 2)
        sub = lax.broadcasted_iota(jnp.int32, (8, NR), 0)
        ka = jnp.broadcast_to(tab[0:1, :], (8, NR))
        ba = jnp.broadcast_to(tab[1:2, :], (8, NR))
        for c in range(5):
            bq, kf = ba * q[c], ka * f2[c]
            ov[c, p + 1, 8:16, :] += jnp.where(sub == 0, (bq + kf) * scale, 0.0)
            ov[c, p + 1, SEC : SEC + 8, :] += jnp.where(sub == 7, (bq - kf) * scale, 0.0)
        return 0

    lax.fori_loop(0, PL, patch, 0)
    outs = [
        pltpu.make_async_copy(ov.at[:, p + 1, 8 : 8 + SEC, :], cyc_out.at[:, p], out_sem.at[p])
        for p in range(PL)
    ]
    for p in range(1, PL - 1):
        outs[p].start()

    for c in axial:
        c.wait_recv()

    def ends(b, _):
        src = pl.ds(pl.multiple_of(b * 8, 8), 8)
        rows = pl.ds(pl.multiple_of((b + 1) * 8, 8), 8)
        q = [qv[c, 0, src, :] for c in range(5)]
        f1 = flux(q, point(q), 1)
        for c in range(5):
            ov[c, 1, rows, :] += BX * (q[c] + f1[c])
        q = [qv[c, PL + 1, src, :] for c in range(5)]
        f1 = flux(q, point(q), 1)
        for c in range(5):
            ov[c, PL, rows, :] = BX * (ov[c, PL, rows, :] + (q[c] - f1[c]))
        return 0

    lax.fori_loop(0, SEC // 8, ends, 0)
    outs[0].start()
    outs[PL - 1].start()

    for c in axial + azim + caxial:
        c.wait_send()

    @pl.when(me > 0)
    def _():
        crow_dn.wait_send()

    @pl.when(me < NA - 1)
    def _():
        crow_up.wait_send()

    for a in range(NA):
        others = [s for s in needed(a) if s != a]

        @pl.when(is_in(me, others))
        def _(a=a):
            tr_copy(a).wait_send()

    def drain(d, _):
        @pl.when(d != me)
        def _():
            sh_copy(d).wait_send()

        return 0

    lax.fori_loop(0, NA, drain, 0)
    core_done.wait()
    for c in outs:
        c.wait()


def body(cycle_state, core_state, core_taps, core_weights, cycle_taps, cycle_weights):
    tab, trig = tables()
    f32, i32 = jnp.float32, jnp.int32
    dma = pltpu.SemaphoreType.DMA
    core_t = jnp.transpose(core_state, (0, 2, 1, 3))
    hbm = pl.BlockSpec(memory_space=pl.ANY)
    vm = pltpu.VMEM
    cycle_new, core_new = pl.pallas_call(
        kernel,
        out_shape=(
            jax.ShapeDtypeStruct(cycle_state.shape, f32),
            jax.ShapeDtypeStruct(core_t.shape, f32),
        ),
        in_specs=[hbm] * 8,
        out_specs=(hbm, hbm),
        scratch_shapes=[
            vm((5, PL + 2, SEC, NR), f32),
            vm((5, PL + 2, SEC + 8, NR), f32),
            vm((5, 2, SEC + 24, 128), f32),
            vm((5, 2, SEC + 24, 128), f32),
            vm((5, PL, 8, NR), f32),
            vm((5, ROWS, PL, NC), f32),
            vm((5, ROWS + 2, PL, 256), f32),
            vm((5, ROWS + 2, PL, 256), f32),
            vm((5, ROWS, PL, NC), f32),
            vm((5, PL, NC), f32),
            vm((5, PL, NC), f32),
            vm((5, ROWS, PL, NC), f32),
            vm((5, 8, 128), f32),
            vm((NA, 5, 8, 128), f32),
            vm((NA, 5, 8, 128), f32),
            vm((NA, 5, 8, 128), f32),
            vm((128, 128), f32),
            vm((5, 8, 128), f32),
            vm((5, 8, 128), f32),
            vm((8, NR), f32),
            vm((8, NT), f32),
            vm((4, 768), i32),
            vm((4, 768), f32),
            vm((4, NT), i32),
            vm((4, NT), f32),
            dma((PL,)),
            dma((7,)),
            dma((PL + 1,)),
            dma((2,)), dma((2,)), dma((2,)), dma((2,)), dma((2,)), dma((2,)), dma((2,)), dma((2,)),
            dma((NA,)), dma((NA,)), dma((NA,)), dma((NA,)),
        ],
        compiler_params=pltpu.CompilerParams(
            collective_id=0, has_side_effects=True, vmem_limit_bytes=60 * 2**20
        ),
    )(cycle_state, core_t, core_taps.T, core_weights.T, cycle_taps.T, cycle_weights.T, tab, trig)
    return cycle_new, jnp.transpose(core_new, (0, 2, 1, 3))


def solution(mesh):
    placed = (P(None, "axial", "azim", None), P(None, "axial", "azim", None), P(), P(), P(), P())
    return jax.shard_map(
        body,
        mesh=mesh,
        in_specs=placed,
        out_specs=(P(None, "axial", "azim", None), P(None, "axial", "azim", None)),
        check_vma=False,
    )
```

```python
import functools
import math

import jax
import jax.numpy as jnp
import numpy as np
from jax import lax
from jax.experimental import pallas as pl
from jax.experimental.pallas import tpu as pltpu
from jax.sharding import PartitionSpec as P

DT = 0.001
DX = 0.004
DR = 1.0 / 256.0
DC = 2.0 / 192.0
NU = 0.002
NT = 2048
NR = 256
NC = 192
PL = 8
SEC = 128
ROWS = 12
W = 16
NA = 16
DA = 2.0 * math.pi / NT

BX = NU * DT / DX**2
AX = DT / (2.0 * DX)
BR = NU * DT / DR**2 / BX
AC = DT / (2.0 * DC) / BX
BC = NU * DT / DC**2 / BX
SX = DX / (2.0 * NU)


def tables():
    radius = lambda i: 1.0 + (i + 0.5) / 256.0
    i = np.arange(NR, dtype=np.float64)
    tab = np.zeros((8, NR))
    tab[0] = DT / (2.0 * DA * radius(i)) / BX
    tab[1] = NU * DT / (DA * radius(i)) ** 2 / BX
    tab[2] = DT * radius(i) / (2.0 * DR * radius(i - 1)) / BX
    tab[3] = DT * radius(i) / (2.0 * DR * radius(i + 1)) / BX
    tab[3, -1] = DT * radius(NR) / (2.0 * DR * radius(NR - 1)) / BX
    tab[4] = 1.0 / BX - 2.0 - 2.0 * BR - 2.0 * tab[1]
    tab[5] = DT / radius(i) / BX
    angle = (np.arange(NT) + 0.5) * (2.0 * math.pi / NT)
    trig = np.zeros((8, NT))
    trig[0] = np.cos(angle)
    trig[1] = np.sin(angle)
    return tab.astype(np.float32), trig.astype(np.float32)


INNER = float(DT * (1.0 - 0.5 / 256.0) / (2.0 * DR * (1.0 + 0.5 / 256.0)) / BX)
CC = float(1.0 / BX - 2.0 - 4.0 * BC)


def needed(a):
    found = set()
    for off in (0, 512):
        found |= {((32 * a - 8 + off) // SEC) % NA, ((32 * a + 37 + off) // SEC) % NA}
    if a == 0:
        found |= set(range(7, 13))
    if a == NA - 1:
        found |= {11, 12, 13, 14, 15, 0}
    return sorted(found)


def fluxes(q):
    inv = pltpu.reciprocal(q[0], approx=False)
    u1, u2, u3 = q[1] * inv, q[2] * inv, q[3] * inv
    p11, p22, p33 = q[1] * u1, q[2] * u2, q[3] * u3
    p12, p13, p23 = q[1] * u2, q[1] * u3, q[2] * u3
    pr = 0.4 * q[4] - 0.2 * (p11 + p22 + p33)
    h = q[4] + pr
    return (
        None,
        [q[1], p11 + pr, p12, p13, h * u1],
        [q[2], p12, p22 + pr, p23, h * u2],
        [q[3], p13, p23, p33 + pr, h * u3],
    )


def kernel(
    cyc, cor, ctaps, cwts, ytaps, ywts, tab_in, trig_in, ov, hal, ah, fix, cres, tab,
    qv, p2s, m2s, cin, cv, oc, chx, crlo, crhi, trs, trr, shs, shr, xm, ep, gl, gr, trig, ct, cw, yt, yw,
    in_sem, sm_sem, ax_s, ax_r, cx_s, cx_r, ar_s, ar_r, cr_s, cr_r, tr_s, tr_r, sh_s, sh_r,
):
    me = lax.axis_index("azim")
    ax = lax.axis_index("axial")
    n_ax = lax.axis_size("axial")
    up_ax = {"axial": lax.rem(ax + 1, n_ax)}
    dn_ax = {"axial": lax.rem(ax + n_ax - 1, n_ax)}
    up_az = {"azim": lax.rem(me + 1, NA)}
    dn_az = {"azim": lax.rem(me + NA - 1, NA)}
    MESH = pl.DeviceIdType.MESH

    barrier = pltpu.get_barrier_semaphore()
    pl.semaphore_signal(barrier, inc=1, device_id=up_ax, device_id_type=MESH)
    pl.semaphore_signal(barrier, inc=1, device_id=dn_ax, device_id_type=MESH)

    def greet(d, _):
        @pl.when(d != me)
        def _():
            pl.semaphore_signal(barrier, inc=1, device_id={"azim": d}, device_id_type=MESH)

        return 0

    lax.fori_loop(0, NA, greet, 0)

    smalls = [
        pltpu.make_async_copy(s, d, sm_sem.at[i])
        for i, (s, d) in enumerate(
            [(cor, cin), (ytaps, yt), (ywts, yw), (tab_in, tab), (trig_in, trig), (ctaps, ct), (cwts, cw)]
        )
    ]
    planes = [pltpu.make_async_copy(cyc.at[:, p], qv.at[:, p], in_sem.at[p]) for p in range(PL)]
    for c in smalls:
        c.start()
    for c in planes:
        c.start()

    def remote(src, dst, s, r, dev):
        return pltpu.make_async_remote_copy(
            src_ref=src, dst_ref=dst, send_sem=s, recv_sem=r, device_id=dev, device_id_type=MESH
        )

    axial = [
        remote(cyc.at[:, 0], hal.at[:, 1], ax_s.at[0], ax_r.at[0], dn_ax),
        remote(cyc.at[:, PL - 1], hal.at[:, 0], ax_s.at[1], ax_r.at[1], up_ax),
    ]
    caxial = [
        remote(cor.at[:, :, 0, :], chx.at[:, :, PL - 1, :], cx_s.at[0], cx_r.at[0], dn_ax),
        remote(cor.at[:, :, PL - 1, :], chx.at[:, :, 0, :], cx_s.at[1], cx_r.at[1], up_ax),
    ]
    azim = [
        remote(cyc.at[:, :, 0, :], ah.at[:, :, 7, :], ar_s.at[0], ar_r.at[0], dn_az),
        remote(cyc.at[:, :, SEC - 1, :], ah.at[:, :, 0, :], ar_s.at[1], ar_r.at[1], up_az),
    ]
    crow_dn = remote(cor.at[:, 0], crhi, cr_s.at[0], cr_r.at[0], dn_az)
    crow_up = remote(cor.at[:, ROWS - 1], crlo, cr_s.at[1], cr_r.at[1], up_az)

    lane8 = lax.broadcasted_iota(jnp.int32, (8, 128), 1)
    row8 = lax.broadcasted_iota(jnp.int32, (8, 128), 0)

    for c in smalls:
        c.wait()
    for i in range(ROWS):
        for c in range(5):
            cv[c, i + 1, :, 0:128] = cin[c, i, :, 0:128]
            cv[c, i + 1, :, 128:192] = cin[c, i, :, 128:192]

    for c in range(5):
        v = jnp.zeros((8, 128), jnp.float32)
        for i in range(ROWS):
            left = pltpu.roll(cv[c, i + 1, :, 0:128], 8 * i, 1)
            right = pltpu.roll(cv[c, i + 1, :, 128:256], (8 * i + 4 - 60) % 128, 1)
            v = jnp.where((lane8 >> 3) == i, jnp.where((lane8 & 7) < 4, left, right), v)
        ep[c, 6] = v

    def bcast(x):
        return jnp.broadcast_to(x, (8, 128))

    def tap_cells(d):
        cols = pl.ds(pl.multiple_of(d * SEC, SEC), SEC)
        ws = [yw[k : k + 1, cols] for k in range(4)]
        total = ws[0] + ws[1] + ws[2] + ws[3]
        cells = []
        for k in range(4):
            tap = bcast(yt[k : k + 1, cols])
            row = ((tap >> 6) * 43691) >> 17
            cells.append((row - me * ROWS, tap - row * NC, bcast(ws[k] / total)))
        return cells

    def share(d, _):
        acc = [jnp.zeros((8, 128), jnp.float32) for _ in range(5)]
        for lrow, col, w in tap_cells(d):
            inside = jnp.logical_and(lrow >= 0, lrow < ROWS)
            side = jnp.logical_or(col < 4, col >= NC - 4)
            idx = (lrow * 8 + jnp.where(col < 4, col, col - (NC - 8))) & 127
            wk = jnp.where(jnp.logical_and(inside, side), w, 0.0)
            for c in range(5):
                acc[c] = acc[c] + wk * jnp.take_along_axis(ep[c, 6], idx, axis=1)
        for c in range(5):
            shs[d, c] = acc[c]
        return 0

    lax.fori_loop(0, NA, share, 0, unroll=4)

    pl.semaphore_wait(barrier, NA - 1 + 2)
    for c in axial:
        c.start()
    for c in azim + caxial:
        c.start()

    @pl.when(me > 0)
    def _():
        crow_dn.start()

    @pl.when(me < NA - 1)
    def _():
        crow_up.start()

    @pl.when(jnp.logical_or(me == 0, me == NA - 1))
    def _():
        r0 = jnp.where(me == 0, 0, ROWS - 4)
        for c in range(5):
            for r in range(4):
                ep[c, r] = cv[c, r0 + r + 1, :, 0:128]
            for j in range(2):
                even = cv[c, r0 + 2 * j + 1, :, 128:256]
                odd = cv[c, r0 + 2 * j + 2, :, 128:256]
                ep[c, 4 + j] = jnp.where(lane8 < 64, even, pltpu.roll(odd, 64, 1))

        def outer(d, _):
            acc = [shs[d, c] for c in range(5)]
            for lrow, col, w in tap_cells(d):
                r = lrow - r0
                mid = jnp.logical_and(col >= 4, col < NC - 4)
                ok = jnp.logical_and(mid, jnp.logical_and(r >= 0, r < 4))
                wk = jnp.where(ok, w, 0.0)
                high = col >= 128
                group = jnp.where(high, 4 + (r >> 1), r)
                idx = jnp.where(high, (col & 63) + ((r & 1) << 6), col) & 127
                for s in range(6):
                    ws = jnp.where(group == s, wk, 0.0)
                    for c in range(5):
                        acc[c] = acc[c] + ws * jnp.take_along_axis(ep[c, s], idx, axis=1)
            for c in range(5):
                shs[d, c] = acc[c]
            return 0

        lax.fori_loop(0, NA, outer, 0, unroll=2)

    def sh_copy(d):
        return remote(shs.at[d], shr.at[me], sh_s.at[d], sh_r.at[me], {"azim": d})

    def send_share(d, _):
        @pl.when(d != me)
        def _():
            sh_copy(d).start()

        return 0

    lax.fori_loop(0, NA, send_share, 0)
    for c in range(5):
        shr[me, c] = shs[me, c]

    for c in planes:
        c.wait()

    lane_s = lax.broadcasted_iota(jnp.int32, (SEC, 128), 1)

    tt = jnp.zeros((SEC, 128), jnp.float32)
    for p in range(PL):
        for c in range(5):
            ch = c * 8 + p
            x = qv[c, p, :, 0:128]
            tt = jnp.where(lane_s == ch, pltpu.roll(x, ch, 1) if ch else x, tt)
    tt = tt.T
    own = pl.ds(pl.multiple_of(me * SEC, SEC), SEC)
    cosine = jnp.broadcast_to(trig[0:1, own], (8, 128))
    sine = jnp.broadcast_to(trig[1:2, own], (8, 128))
    tq = [tt[8 * c : 8 * c + 8, :] for c in range(5)]
    cart = [tq[0], tq[1], tq[3] * cosine - tq[2] * sine, tq[3] * sine + tq[2] * cosine, tq[4]]
    for c in range(5):
        trs[c] = cart[c]
        trr[me, c] = cart[c]

    def tr_copy(d):
        return remote(trs, trr.at[me], tr_s.at[d], tr_r.at[me], {"azim": d})

    def is_in(x, items):
        hit = x == items[0]
        for it in items[1:]:
            hit = jnp.logical_or(hit, x == it)
        return hit

    for a in range(NA):
        others = [s for s in needed(a) if s != a]

        @pl.when(is_in(me, others))
        def _(a=a):
            tr_copy(a).start()

    first, last = lane8 == 0, lane8 == 127
    zero8 = jnp.zeros((8, 128), jnp.float32)
    wide_first = lax.broadcasted_iota(jnp.int32, (W, 128), 1) == 0
    wide_last = lax.broadcasted_iota(jnp.int32, (W, 128), 1) == 127
    for c in range(5):
        for h in range(2):
            m2s[c, h, 2 * W - 8 : 2 * W, :] = zero8
            p2s[c, h, 2 * W + SEC : 2 * W + SEC + 8, :] = zero8
        ov[c, 1, W : W + SEC, :] = jnp.zeros((SEC, NR), jnp.float32)

    def cycle_plane(p, _):
        for b in range(SEC // W + 1):
            rows, prev, now = pl.ds(W * b + W, W), pl.ds(W * b, W), pl.ds(W * b + 2 * W, W)
            if b < SEC // W:
                q = [qv[c, p, W * b : W * b + W, :] for c in range(5)]
                _, f1, f2, f3 = fluxes(q)
                row = lambda k: jnp.broadcast_to(tab[k : k + 1, :], (W, NR))
                ka, ba, cp, cm, cc, so = [row(k) for k in range(6)]
                for c in range(5):
                    ov[c, p, rows, :] += q[c] - f1[c]
                    acc = ov[c, p + 1, rows, :] + cc * q[c]
                    ov[c, p + 2, rows, :] = q[c] + f1[c]
                    base = BR * q[c]
                    p3 = base - cp * f3[c]
                    m3 = base + cm * f3[c]
                    pl0, pl1 = pltpu.roll(p3[:, :128], 127, 1), pltpu.roll(p3[:, 128:], 127, 1)
                    ml0, ml1 = pltpu.roll(m3[:, :128], 1, 1), pltpu.roll(m3[:, 128:], 1, 1)
                    wall = m3[:, 128:] if c != 3 else -m3[:, 128:]
                    lo = jnp.where(wide_last, pl1, pl0) + jnp.where(wide_first, 0.0, ml0)
                    hi = jnp.where(wide_last, wall, pl1) + jnp.where(wide_first, ml0, ml1)
                    acc = acc + jnp.concatenate([lo, hi], axis=1)
                    if c == 2:
                        acc = acc - so * f2[3]
                    if c == 3:
                        acc = acc + so * f2[2]
                    ov[c, p + 1, rows, :] = acc
                    bq, kf = ba * q[c], ka * f2[c]
                    p2, m2 = bq - kf, bq + kf
                    for h in range(2):
                        half = slice(128 * h, 128 * h + 128)
                        p2s[c, h, now, :] = p2[:, half]
                        m2s[c, h, now, :] = m2[:, half]
            if b:
                for c in range(5):
                    for h in range(2):
                        half = slice(128 * h, 128 * h + 128)
                        up = p2s[c, h, pl.ds(W * b + W + 1, W), :]
                        dn = m2s[c, h, pl.ds(W * b + W - 1, W), :]
                        ov[c, p + 1, prev, half] += up + dn
        return 0

    lax.fori_loop(0, PL, cycle_plane, 0)

    for s in range(NA):
        takers = [a for a in range(NA) if s in needed(a) and a != s]

        @pl.when(is_in(me, takers))
        def _(s=s):
            remote(trs, trr.at[s], tr_s.at[s], tr_r.at[s], {"azim": s}).wait_recv()

    s0 = ((32 * me + 2040) >> 7) & 15
    s1 = ((32 * me + 37) >> 7) & 15

    def ghost(start, shift, sectors):
        vals = [zero8 for _ in range(5)]
        ws = [bcast_roll(cw[k : k + 1, start : start + 256], shift) for k in range(4)]
        total = ws[0] + ws[1] + ws[2] + ws[3]
        for k in range(4):
            tap = bcast_roll(ct[k : k + 1, start : start + 256], shift)
            idx = tap & 127
            sec = tap >> 7
            w = ws[k] / total
            for c in range(5):
                v = jnp.take_along_axis(trr[sectors[0], c], idx, axis=1)
                for s in sectors[1:]:
                    v = jnp.where(sec == s, jnp.take_along_axis(trr[s, c], idx, axis=1), v)
                vals[c] = vals[c] + w * v
        return vals

    def bcast_roll(x, shift):
        full = jnp.broadcast_to(x, (8, 256))
        if isinstance(shift, int):
            return full[:, shift : shift + 128]
        return pltpu.roll(full, shift, 1)[:, :128]

    def col_terms(g):
        return fluxes(g)[3]

    back = lax.rem(512 - ROWS * me, 256)
    g = ghost(0, back, [s0, s1])
    f = col_terms(g)
    for c in range(5):
        gl[c] = BC * g[c] + AC * f[c]
    back = lax.rem(512 - 64 - ROWS * me, 256)
    g = ghost(128, back, [(s0 + 4) & 15, (s1 + 4) & 15])
    f = col_terms(g)
    for c in range(5):
        gr[c] = BC * g[c] - AC * f[c]

    @pl.when(me > 0)
    def _():
        crow_up.wait_recv()
        for c in range(5):
            cv[c, 0, :, 0:128] = crlo[c, :, 0:128]
            cv[c, 0, :, 128:192] = crlo[c, :, 128:192]

    @pl.when(me < NA - 1)
    def _():
        crow_dn.wait_recv()
        for c in range(5):
            cv[c, ROWS + 1, :, 0:128] = crhi[c, :, 0:128]
            cv[c, ROWS + 1, :, 128:192] = crhi[c, :, 128:192]

    @pl.when(me == 0)
    def _():
        for h in range(2):
            g = ghost(384, 0, list(range(7, 13))) if h == 0 else ghost(384, 128, list(range(7, 13)))
            for c in range(5):
                cv[c, 0, :, 128 * h : 128 * h + 128] = g[c]

    @pl.when(me == NA - 1)
    def _():
        g = ghost(512, 64, [11, 12, 13, 14, 15, 0])
        for c in range(5):
            cv[c, ROWS + 1, :, 0:128] = g[c]
        g = ghost(512, 128, [11, 12, 13, 14, 15, 0])
        for c in range(5):
            cv[c, ROWS + 1, :, 128:256] = pltpu.roll(g[c], 64, 1)

    for c in caxial:
        c.wait_recv()

    sub = lax.broadcasted_iota(jnp.int32, (8, 256), 0)
    q = [cv[c, 0, :, :] for c in range(5)]
    f2 = fluxes(q)[2]
    for c in range(5):
        oc[c, 1] = BC * q[c] + AC * f2[c]
    for i in range(1, ROWS + 1):
        q = [cv[c, i, :, :] for c in range(5)]
        _, f1, f2, f3 = fluxes(q)
        x = [chx[c, i - 1, :, :] for c in range(5)]
        x = [jnp.concatenate([v, jnp.ones((8, 64), jnp.float32)], axis=1) for v in x]
        xf = fluxes(x)[1]
        for c in range(5):
            m1 = pltpu.roll(q[c] + f1[c], 1, 0)
            p1 = pltpu.roll(q[c] - f1[c], 7, 0)
            m1 = jnp.where(sub == 0, x[c] + xf[c], m1)
            p1 = jnp.where(sub == 7, x[c] - xf[c], p1)
            acc = oc[c, i] + CC * q[c] + m1 + p1
            base = BC * q[c]
            p3, m3 = base - AC * f3[c], base + AC * f3[c]
            a, bb = pltpu.roll(p3[:, :128], 127, 1), pltpu.roll(p3[:, 128:], 127, 1)
            e, f = pltpu.roll(m3[:, :128], 1, 1), pltpu.roll(m3[:, 128:], 1, 1)
            lg = pltpu.roll(gl[c], 129 - i, 1) if i > 1 else gl[c]
            rg = pltpu.roll(gr[c], 64 - i, 1)
            lo = jnp.where(last, bb, a) + jnp.where(first, lg, e)
            hi = jnp.where(lane8 == 63, rg, bb) + jnp.where(first, e, f)
            acc = acc + jnp.concatenate([lo, hi], axis=1)
            p2, m2 = base - AC * f2[c], base + AC * f2[c]
            if i > 1:
                done = BX * (oc[c, i - 1] + p2)
                cres[c, i - 2, :, 0:128] = done[:, 0:128]
                cres[c, i - 2, :, 128:192] = done[:, 128:192]
            oc[c, i] = acc
            if i < ROWS:
                oc[c, i + 1] = m2
    q = [cv[c, ROWS + 1, :, :] for c in range(5)]
    f2 = fluxes(q)[2]
    for c in range(5):
        done = BX * (oc[c, ROWS] + BC * q[c] - AC * f2[c])
        cres[c, ROWS - 1, :, 0:128] = done[:, 0:128]
        cres[c, ROWS - 1, :, 128:192] = done[:, 128:192]

    def await_share(d, _):
        @pl.when(d != me)
        def _():
            remote(shs.at[d], shr.at[d], sh_s.at[d], sh_r.at[d], {"azim": d}).wait_recv()

        return 0

    lax.fori_loop(0, NA, await_share, 0)
    cart = [functools.reduce(jnp.add, [shr[d, c] for d in range(NA)]) for c in range(5)]
    g = [cart[0], cart[1], cart[3] * cosine - cart[2] * sine, cart[2] * cosine + cart[3] * sine, cart[4]]
    f3 = fluxes(g)[3]
    for c in range(5):
        xm[8 * c : 8 * c + 8, :] = BR * g[c] + INNER * f3[c]
    fix[...] = xm[...].T
    for c in azim + axial:
        c.wait_recv()

    for c in axial + azim + caxial:
        c.wait_send()

    @pl.when(me > 0)
    def _():
        crow_dn.wait_send()

    @pl.when(me < NA - 1)
    def _():
        crow_up.wait_send()

    for a in range(NA):
        others = [s for s in needed(a) if s != a]

        @pl.when(is_in(me, others))
        def _(a=a):
            tr_copy(a).wait_send()

    def drain(d, _):
        @pl.when(d != me)
        def _():
            sh_copy(d).wait_send()

        return 0

    lax.fori_loop(0, NA, drain, 0)


def closing(ov, hal, ah, fix, core, tab, cyc_out, cor_out, buf, sems):
    core_copy = pltpu.make_async_copy(core, cor_out, sems.at[PL])
    core_copy.start()
    top = lax.broadcasted_iota(jnp.int32, (8, NR), 0) == 0
    bottom = lax.broadcasted_iota(jnp.int32, (8, NR), 0) == 7
    first = lax.broadcasted_iota(jnp.int32, (W, 128), 1) == 0
    ka = jnp.broadcast_to(tab[0:1, :], (8, NR))
    ba = jnp.broadcast_to(tab[1:2, :], (8, NR))

    def copy(p):
        return pltpu.make_async_copy(buf.at[:, p], cyc_out.at[:, p], sems.at[p])

    def plane(p, axial):
        side = [ah[c, p, :, :] for c in range(5)]
        f2 = fluxes(side)[2]
        lo = [jnp.where(top, ba * side[c] + ka * f2[c], 0.0) for c in range(5)]
        hi = [jnp.where(bottom, ba * side[c] - ka * f2[c], 0.0) for c in range(5)]
        for b in range(SEC // W):
            rows = slice(W * b, W * b + W)
            if axial is not None:
                q = [hal[c, axial, rows, :] for c in range(5)]
                f1 = fluxes(q)[1]
            inner = fix[rows, :]
            for c in range(5):
                v = ov[c, p + 1, W * b + W : W * b + 2 * W, :]
                if axial == 0:
                    v = v + (q[c] + f1[c])
                if axial == 1:
                    v = v + (q[c] - f1[c])
                if b == 0:
                    v = jnp.concatenate([v[:8] + lo[c], v[8:]], axis=0)
                if b == SEC // W - 1:
                    v = jnp.concatenate([v[: W - 8], v[W - 8 :] + hi[c]], axis=0)
                col = jnp.where(first, pltpu.roll(inner, lax.rem(128 - 8 * c - p, 128), 1), 0.0)
                buf[c, p, rows, 0:128] = BX * (v[:, :128] + col)
                buf[c, p, rows, 128:256] = BX * v[:, 128:]
        copy(p).start()

    def middle(p, _):
        plane(p, None)
        return 0

    lax.fori_loop(1, PL - 1, middle, 0)
    plane(jnp.int32(0), 0)
    plane(jnp.int32(PL - 1), 1)
    core_copy.wait()
    for p in range(PL):
        copy(p).wait()


def body(cycle_state, core_state, core_taps, core_weights, cycle_taps, cycle_weights):
    tab, trig = tables()
    f32, i32 = jnp.float32, jnp.int32
    dma = pltpu.SemaphoreType.DMA
    core_t = jnp.transpose(core_state, (0, 2, 1, 3))
    hbm = pl.BlockSpec(memory_space=pltpu.HBM)
    vmem = pl.BlockSpec(memory_space=pltpu.VMEM)
    vm = pltpu.VMEM
    shape = lambda *dims: jax.ShapeDtypeStruct(dims, f32)
    operands = [
        pltpu.with_memory_space_constraint(x, pltpu.HBM)
        for x in (
            cycle_state, core_t, core_taps.T, core_weights.T, cycle_taps.T, cycle_weights.T,
            jnp.asarray(tab), jnp.asarray(trig),
        )
    ]
    parts = pl.pallas_call(
        kernel,
        out_shape=(
            shape(5, PL + 2, SEC + W, NR),
            shape(5, 2, SEC, NR),
            shape(5, PL, 8, NR),
            shape(128, 128),
            shape(5, ROWS, PL, NC),
            shape(8, NR),
        ),
        in_specs=[hbm] * 8,
        out_specs=(vmem,) * 6,
        scratch_shapes=[
            vm((5, PL, SEC, NR), f32),
            vm((5, 2, SEC + 4 * W, 128), f32),
            vm((5, 2, SEC + 4 * W, 128), f32),
            vm((5, ROWS, PL, NC), f32),
            vm((5, ROWS + 2, PL, 256), f32),
            vm((5, ROWS + 2, PL, 256), f32),
            vm((5, ROWS, PL, NC), f32),
            vm((5, PL, NC), f32),
            vm((5, PL, NC), f32),
            vm((5, 8, 128), f32),
            vm((NA, 5, 8, 128), f32),
            vm((NA, 5, 8, 128), f32),
            vm((NA, 5, 8, 128), f32),
            vm((128, 128), f32),
            vm((5, 7, 8, 128), f32),
            vm((5, 8, 128), f32),
            vm((5, 8, 128), f32),
            vm((8, NT), f32),
            vm((4, 768), i32),
            vm((4, 768), f32),
            vm((4, NT), i32),
            vm((4, NT), f32),
            dma((PL,)),
            dma((7,)),
            dma((2,)), dma((2,)), dma((2,)), dma((2,)), dma((2,)), dma((2,)), dma((2,)), dma((2,)),
            dma((NA,)), dma((NA,)), dma((NA,)), dma((NA,)),
        ],
        compiler_params=pltpu.CompilerParams(
            collective_id=0, has_side_effects=True, vmem_limit_bytes=24 * 2**20
        ),
    )(*operands)
    cycle_new, core_new = pl.pallas_call(
        closing,
        out_shape=(
            jax.ShapeDtypeStruct(cycle_state.shape, f32),
            jax.ShapeDtypeStruct(core_t.shape, f32),
        ),
        in_specs=[vmem] * 6,
        out_specs=(hbm, hbm),
        scratch_shapes=[vm((5, PL, SEC, NR), f32), dma((PL + 1,))],
        compiler_params=pltpu.CompilerParams(vmem_limit_bytes=12 * 2**20),
    )(*parts)
    return cycle_new, jnp.transpose(core_new, (0, 2, 1, 3))


def solution(mesh):
    placed = (P(None, "axial", "azim", None), P(None, "axial", "azim", None), P(), P(), P(), P())
    return jax.shard_map(
        body,
        mesh=mesh,
        in_specs=placed,
        out_specs=(P(None, "axial", "azim", None), P(None, "axial", "azim", None)),
        check_vma=False,
    )
```

```python
import functools
import math

import jax
import jax.numpy as jnp
import numpy as np
from jax import lax
from jax.experimental import pallas as pl
from jax.experimental.pallas import tpu as pltpu
from jax.sharding import PartitionSpec as P

DT = 0.001
DX = 0.004
DR = 1.0 / 256.0
DC = 2.0 / 192.0
NU = 0.002
NT = 2048
NR = 256
NC = 192
PL = 8
SEC = 128
ROWS = 12
W = 16
NA = 16
HUB = NA - 1
DA = 2.0 * math.pi / NT

BX = NU * DT / DX**2
AX = DT / (2.0 * DX)
BR = NU * DT / DR**2 / BX
AC = DT / (2.0 * DC) / BX
BC = NU * DT / DC**2 / BX
SX = DX / (2.0 * NU)


def tables():
    radius = lambda i: 1.0 + (i + 0.5) / 256.0
    i = np.arange(NR, dtype=np.float64)
    tab = np.zeros((8, NR))
    tab[0] = DT / (2.0 * DA * radius(i)) / BX
    tab[1] = NU * DT / (DA * radius(i)) ** 2 / BX
    tab[2] = DT * radius(i) / (2.0 * DR * radius(i - 1)) / BX
    tab[3] = DT * radius(i) / (2.0 * DR * radius(i + 1)) / BX
    tab[3, -1] = DT * radius(NR) / (2.0 * DR * radius(NR - 1)) / BX
    tab[4] = 1.0 / BX - 2.0 - 2.0 * BR - 2.0 * tab[1]
    tab[5] = DT / radius(i) / BX
    angle = (np.arange(NT) + 0.5) * (2.0 * math.pi / NT)
    trig = np.zeros((8, NT))
    trig[0] = np.cos(angle)
    trig[1] = np.sin(angle)
    return tab.astype(np.float32), trig.astype(np.float32)


INNER = float(DT * (1.0 - 0.5 / 256.0) / (2.0 * DR * (1.0 + 0.5 / 256.0)) / BX)
CC = float(1.0 / BX - 2.0 - 4.0 * BC)


def needed(a):
    found = set()
    for off in (0, 512):
        found |= {((32 * a - 8 + off) // SEC) % NA, ((32 * a + 37 + off) // SEC) % NA}
    if a == 0:
        found |= set(range(7, 13))
    if a == NA - 1:
        found |= {11, 12, 13, 14, 15, 0}
    return sorted(found)


def fluxes(q):
    inv = pltpu.reciprocal(q[0], approx=False)
    u1, u2, u3 = q[1] * inv, q[2] * inv, q[3] * inv
    p11, p22, p33 = q[1] * u1, q[2] * u2, q[3] * u3
    p12, p13, p23 = q[1] * u2, q[1] * u3, q[2] * u3
    pr = 0.4 * q[4] - 0.2 * (p11 + p22 + p33)
    h = q[4] + pr
    return (
        None,
        [q[1], p11 + pr, p12, p13, h * u1],
        [q[2], p12, p22 + pr, p23, h * u2],
        [q[3], p13, p23, p33 + pr, h * u3],
    )


def kernel(
    cyc, cor, ctaps, cwts, ytaps, ywts, tab_in, trig_in, ov, hal, ah, fix, cres, tab,
    qv, p2s, m2s, cin, cv, oc, chx, crlo, crhi, trs, trr, shs, shr, xm, ep, gl, gr, trig, ct, cw, yt, yw,
    all_in, in_sem, sm_sem, ax_s, ax_r, cx_s, cx_r, ar_s, ar_r, cr_s, cr_r, tr_s, tr_r, sh_s, sh_r,
):
    me = lax.axis_index("azim")
    ax = lax.axis_index("axial")
    n_ax = lax.axis_size("axial")
    up_ax = {"axial": lax.rem(ax + 1, n_ax)}
    dn_ax = {"axial": lax.rem(ax + n_ax - 1, n_ax)}
    up_az = {"azim": lax.rem(me + 1, NA)}
    dn_az = {"azim": lax.rem(me + NA - 1, NA)}
    MESH = pl.DeviceIdType.MESH

    barrier = pltpu.get_barrier_semaphore()
    pl.semaphore_signal(barrier, inc=1, device_id=up_ax, device_id_type=MESH)
    pl.semaphore_signal(barrier, inc=1, device_id=dn_ax, device_id_type=MESH)

    @pl.when(jnp.logical_and(me != HUB, me != 0))
    def _():
        pl.semaphore_signal(barrier, inc=1, device_id={"azim": HUB}, device_id_type=MESH)

    def greet(d, _):
        pl.semaphore_signal(barrier, inc=1, device_id={"azim": d}, device_id_type=MESH)
        return 0

    lax.fori_loop(1, jnp.where(me == 0, NA, 1), greet, 0)

    smalls = [
        pltpu.make_async_copy(s, d, sm_sem.at[i])
        for i, (s, d) in enumerate(
            [(cor, cin), (ytaps, yt), (ywts, yw), (tab_in, tab), (trig_in, trig), (ctaps, ct), (cwts, cw)]
        )
    ]
    planes = [pltpu.make_async_copy(cyc.at[:, p], qv.at[:, p], in_sem.at[p]) for p in range(PL)]
    for c in smalls:
        c.start()
    for c in planes:
        c.start()

    def remote(src, dst, s, r, dev):
        return pltpu.make_async_remote_copy(
            src_ref=src, dst_ref=dst, send_sem=s, recv_sem=r, device_id=dev, device_id_type=MESH
        )

    axial = [
        remote(cyc.at[:, 0], hal.at[:, 1], ax_s.at[0], ax_r.at[0], dn_ax),
        remote(cyc.at[:, PL - 1], hal.at[:, 0], ax_s.at[1], ax_r.at[1], up_ax),
    ]
    caxial = [
        remote(cor.at[:, :, 0, :], chx.at[:, :, PL - 1, :], cx_s.at[0], cx_r.at[0], dn_ax),
        remote(cor.at[:, :, PL - 1, :], chx.at[:, :, 0, :], cx_s.at[1], cx_r.at[1], up_ax),
    ]
    azim = [
        remote(cyc.at[:, :, 0, :], ah.at[:, :, 7, :], ar_s.at[0], ar_r.at[0], dn_az),
        remote(cyc.at[:, :, SEC - 1, :], ah.at[:, :, 0, :], ar_s.at[1], ar_r.at[1], up_az),
    ]
    crow_dn = remote(cor.at[:, 0], crhi, cr_s.at[0], cr_r.at[0], dn_az)
    crow_up = remote(cor.at[:, ROWS - 1], crlo, cr_s.at[1], cr_r.at[1], up_az)

    lane8 = lax.broadcasted_iota(jnp.int32, (8, 128), 1)
    row8 = lax.broadcasted_iota(jnp.int32, (8, 128), 0)

    def prepare():
        for c in smalls:
            c.wait()
        for i in range(ROWS):
            for c in range(5):
                cv[c, i + 1, :, 0:128] = cin[c, i, :, 0:128]
                cv[c, i + 1, :, 128:192] = cin[c, i, :, 128:192]

        for c in range(5):
            v = jnp.zeros((8, 128), jnp.float32)
            for i in range(ROWS):
                left = pltpu.roll(cv[c, i + 1, :, 0:128], 8 * i, 1)
                right = pltpu.roll(cv[c, i + 1, :, 128:256], (8 * i + 4 - 60) % 128, 1)
                v = jnp.where((lane8 >> 3) == i, jnp.where((lane8 & 7) < 4, left, right), v)
            ep[c, 6] = v

    @pl.when(ax < 2)
    def _():
        prepare()

    pl.semaphore_wait(barrier, 2 + jnp.where(me == HUB, NA - 1, jnp.where(me == 0, 0, 1)))
    for c in axial + caxial:
        c.start()

    def tell(d, _):
        pl.semaphore_signal(all_in, inc=1, device_id={"azim": d}, device_id_type=MESH)
        return 0

    lax.fori_loop(0, jnp.where(me == HUB, NA - 1, 0), tell, 0)

    @pl.when(ax >= 2)
    def _():
        prepare()

    def bcast(x):
        return jnp.broadcast_to(x, (8, 128))

    def tap_cells(d):
        cols = pl.ds(pl.multiple_of(d * SEC, SEC), SEC)
        ws = [yw[k : k + 1, cols] for k in range(4)]
        total = ws[0] + ws[1] + ws[2] + ws[3]
        cells = []
        for k in range(4):
            tap = bcast(yt[k : k + 1, cols])
            row = ((tap >> 6) * 43691) >> 17
            cells.append((row - me * ROWS, tap - row * NC, bcast(ws[k] / total)))
        return cells

    def share(d, _):
        acc = [jnp.zeros((8, 128), jnp.float32) for _ in range(5)]
        for lrow, col, w in tap_cells(d):
            inside = jnp.logical_and(lrow >= 0, lrow < ROWS)
            side = jnp.logical_or(col < 4, col >= NC - 4)
            idx = (lrow * 8 + jnp.where(col < 4, col, col - (NC - 8))) & 127
            wk = jnp.where(jnp.logical_and(inside, side), w, 0.0)
            for c in range(5):
                acc[c] = acc[c] + wk * jnp.take_along_axis(ep[c, 6], idx, axis=1)
        for c in range(5):
            shs[d, c] = acc[c]
        return 0

    lax.fori_loop(0, NA, share, 0, unroll=4)

    r0 = jnp.where(me == 0, 0, ROWS - 4)

    @pl.when(jnp.logical_or(me == 0, me == NA - 1))
    def _():
        for c in range(5):
            for r in range(4):
                ep[c, r] = cv[c, r0 + r + 1, :, 0:128]
            for j in range(2):
                even = cv[c, r0 + 2 * j + 1, :, 128:256]
                odd = cv[c, r0 + 2 * j + 2, :, 128:256]
                ep[c, 4 + j] = jnp.where(lane8 < 64, even, pltpu.roll(odd, 64, 1))

    def outer(d, _):
        acc = [shs[d, c] for c in range(5)]
        for lrow, col, w in tap_cells(d):
            r = lrow - r0
            mid = jnp.logical_and(col >= 4, col < NC - 4)
            ok = jnp.logical_and(mid, jnp.logical_and(r >= 0, r < 4))
            wk = jnp.where(ok, w, 0.0)
            high = col >= 128
            group = jnp.where(high, 4 + (r >> 1), r)
            idx = jnp.where(high, (col & 63) + ((r & 1) << 6), col) & 127
            for s in range(6):
                ws = jnp.where(group == s, wk, 0.0)
                for c in range(5):
                    acc[c] = acc[c] + ws * jnp.take_along_axis(ep[c, s], idx, axis=1)
        for c in range(5):
            shs[d, c] = acc[c]
        return 0


    def sh_copy(d):
        return remote(shs.at[d], shr.at[me], sh_s.at[d], sh_r.at[me], {"azim": d})

    def send_share(d, _):
        @pl.when(d != me)
        def _():
            sh_copy(d).start()

        return 0

    def outer_and_send(d, _):
        outer(d, 0)
        return send_share(d, 0)

    lane_s = lax.broadcasted_iota(jnp.int32, (SEC, 128), 1)
    own = pl.ds(pl.multiple_of(me * SEC, SEC), SEC)
    cosine = jnp.broadcast_to(trig[0:1, own], (8, 128))
    sine = jnp.broadcast_to(trig[1:2, own], (8, 128))

    def trace():
        for c in planes:
            c.wait()
        tt = jnp.zeros((SEC, 128), jnp.float32)
        for p in range(PL):
            for c in range(5):
                ch = c * 8 + p
                x = qv[c, p, :, 0:128]
                tt = jnp.where(lane_s == ch, pltpu.roll(x, ch, 1) if ch else x, tt)
        tt = tt.T
        tq = [tt[8 * c : 8 * c + 8, :] for c in range(5)]
        cart = [tq[0], tq[1], tq[3] * cosine - tq[2] * sine, tq[3] * sine + tq[2] * cosine, tq[4]]
        for c in range(5):
            trs[c] = cart[c]
            trr[me, c] = cart[c]

    first, last = lane8 == 0, lane8 == 127
    zero8 = jnp.zeros((8, 128), jnp.float32)
    wide_first = lax.broadcasted_iota(jnp.int32, (W, 128), 1) == 0
    wide_last = lax.broadcasted_iota(jnp.int32, (W, 128), 1) == 127
    for c in range(5):
        for h in range(2):
            m2s[c, h, 2 * W - 8 : 2 * W, :] = zero8
            p2s[c, h, 2 * W + SEC : 2 * W + SEC + 8, :] = zero8
        ov[c, 1, W : W + SEC, :] = jnp.zeros((SEC, NR), jnp.float32)

    def cycle_plane(p, _):
        for b in range(SEC // W + 1):
            rows, prev, now = pl.ds(W * b + W, W), pl.ds(W * b, W), pl.ds(W * b + 2 * W, W)
            if b < SEC // W:
                q = [qv[c, p, W * b : W * b + W, :] for c in range(5)]
                _, f1, f2, f3 = fluxes(q)
                row = lambda k: jnp.broadcast_to(tab[k : k + 1, :], (W, NR))
                ka, ba, cp, cm, cc, so = [row(k) for k in range(6)]
                for c in range(5):
                    ov[c, p, rows, :] += q[c] - f1[c]
                    acc = ov[c, p + 1, rows, :] + cc * q[c]
                    ov[c, p + 2, rows, :] = q[c] + f1[c]
                    base = BR * q[c]
                    p3 = base - cp * f3[c]
                    m3 = base + cm * f3[c]
                    pl0, pl1 = pltpu.roll(p3[:, :128], 127, 1), pltpu.roll(p3[:, 128:], 127, 1)
                    ml0, ml1 = pltpu.roll(m3[:, :128], 1, 1), pltpu.roll(m3[:, 128:], 1, 1)
                    wall = m3[:, 128:] if c != 3 else -m3[:, 128:]
                    lo = jnp.where(wide_last, pl1, pl0) + jnp.where(wide_first, 0.0, ml0)
                    hi = jnp.where(wide_last, wall, pl1) + jnp.where(wide_first, ml0, ml1)
                    acc = acc + jnp.concatenate([lo, hi], axis=1)
                    if c == 2:
                        acc = acc - so * f2[3]
                    if c == 3:
                        acc = acc + so * f2[2]
                    ov[c, p + 1, rows, :] = acc
                    bq, kf = ba * q[c], ka * f2[c]
                    p2, m2 = bq - kf, bq + kf
                    for h in range(2):
                        half = slice(128 * h, 128 * h + 128)
                        p2s[c, h, now, :] = p2[:, half]
                        m2s[c, h, now, :] = m2[:, half]
            if b:
                for c in range(5):
                    for h in range(2):
                        half = slice(128 * h, 128 * h + 128)
                        up = p2s[c, h, pl.ds(W * b + W + 1, W), :]
                        dn = m2s[c, h, pl.ds(W * b + W - 1, W), :]
                        ov[c, p + 1, prev, half] += up + dn
        return 0

    ahead = jnp.where(me == 0, 0, jnp.maximum((12 - me) // 4, 0))
    trace()

    @pl.when(me == 0)
    def _():
        lax.fori_loop(0, NA, outer, 0, unroll=2)

    def tr_copy(d):
        return remote(trs, trr.at[me], tr_s.at[d], tr_r.at[me], {"azim": d})

    def is_in(x, items):
        hit = x == items[0]
        for it in items[1:]:
            hit = jnp.logical_or(hit, x == it)
        return hit

    between = jnp.logical_and(me != 0, me != HUB)

    @pl.when(jnp.logical_and(between, is_in(me, [s for s in needed(0) if s])))
    def _():
        tr_copy(0).start()

    @pl.when(between)
    def _():
        sh_copy(0).start()

    lax.fori_loop(0, ahead, cycle_plane, 0)

    @pl.when(me != HUB)
    def _():
        pl.semaphore_wait(all_in, 1)

    for a in range(NA):
        others = [s for s in needed(a) if s != a]

        @pl.when(is_in(me, [HUB] if a == 0 else others))
        def _(a=a):
            tr_copy(a).start()

    for c in azim:
        c.start()

    @pl.when(me > 0)
    def _():
        crow_dn.start()

    @pl.when(me < NA - 1)
    def _():
        crow_up.start()

    @pl.when(me == NA - 1)
    def _():
        lax.fori_loop(0, NA, outer_and_send, 0)

    @pl.when(me != NA - 1)
    def _():
        lax.fori_loop(1, NA, send_share, 0)

    for c in range(5):
        shr[me, c] = shs[me, c]

    lax.fori_loop(ahead, PL, cycle_plane, 0)

    for s in range(NA):
        takers = [a for a in range(NA) if s in needed(a) and a != s]

        @pl.when(is_in(me, takers))
        def _(s=s):
            remote(trs, trr.at[s], tr_s.at[s], tr_r.at[s], {"azim": s}).wait_recv()

    s0 = ((32 * me + 2040) >> 7) & 15
    s1 = ((32 * me + 37) >> 7) & 15

    def ghost(start, shift, sectors):
        vals = [zero8 for _ in range(5)]
        ws = [bcast_roll(cw[k : k + 1, start : start + 256], shift) for k in range(4)]
        total = ws[0] + ws[1] + ws[2] + ws[3]
        for k in range(4):
            tap = bcast_roll(ct[k : k + 1, start : start + 256], shift)
            idx = tap & 127
            sec = tap >> 7
            w = ws[k] / total
            for c in range(5):
                v = jnp.take_along_axis(trr[sectors[0], c], idx, axis=1)
                for s in sectors[1:]:
                    v = jnp.where(sec == s, jnp.take_along_axis(trr[s, c], idx, axis=1), v)
                vals[c] = vals[c] + w * v
        return vals

    def bcast_roll(x, shift):
        full = jnp.broadcast_to(x, (8, 256))
        if isinstance(shift, int):
            return (pltpu.roll(full, 256 - shift, 1) if shift else full)[:, :128]
        return pltpu.roll(full, shift, 1)[:, :128]

    def col_terms(g):
        return fluxes(g)[3]

    back = lax.rem(512 - ROWS * me, 256)
    g = ghost(0, back, [s0, s1])
    f = col_terms(g)
    for c in range(5):
        gl[c] = BC * g[c] + AC * f[c]
    back = lax.rem(512 - 64 - ROWS * me, 256)
    g = ghost(128, back, [(s0 + 4) & 15, (s1 + 4) & 15])
    f = col_terms(g)
    for c in range(5):
        gr[c] = BC * g[c] - AC * f[c]

    @pl.when(me > 0)
    def _():
        crow_up.wait_recv()
        for c in range(5):
            cv[c, 0, :, 0:128] = crlo[c, :, 0:128]
            cv[c, 0, :, 128:192] = crlo[c, :, 128:192]

    @pl.when(me < NA - 1)
    def _():
        crow_dn.wait_recv()
        for c in range(5):
            cv[c, ROWS + 1, :, 0:128] = crhi[c, :, 0:128]
            cv[c, ROWS + 1, :, 128:192] = crhi[c, :, 128:192]

    @pl.when(me == 0)
    def _():
        for h in range(2):
            g = ghost(384, 0, list(range(7, 13))) if h == 0 else ghost(384, 128, list(range(7, 13)))
            for c in range(5):
                cv[c, 0, :, 128 * h : 128 * h + 128] = g[c]

    @pl.when(me == NA - 1)
    def _():
        g = ghost(512, 64, [11, 12, 13, 14, 15, 0])
        for c in range(5):
            cv[c, ROWS + 1, :, 0:128] = g[c]
        g = ghost(512, 192, [11, 12, 13, 14, 15, 0])
        for c in range(5):
            cv[c, ROWS + 1, :, 128:256] = g[c]

    for c in caxial:
        c.wait_recv()

    sub = lax.broadcasted_iota(jnp.int32, (8, 256), 0)
    q = [cv[c, 0, :, :] for c in range(5)]
    f2 = fluxes(q)[2]
    for c in range(5):
        oc[c, 1] = BC * q[c] + AC * f2[c]
    for i in range(1, ROWS + 1):
        q = [cv[c, i, :, :] for c in range(5)]
        _, f1, f2, f3 = fluxes(q)
        x = [chx[c, i - 1, :, :] for c in range(5)]
        x = [jnp.concatenate([v, jnp.ones((8, 64), jnp.float32)], axis=1) for v in x]
        xf = fluxes(x)[1]
        for c in range(5):
            m1 = pltpu.roll(q[c] + f1[c], 1, 0)
            p1 = pltpu.roll(q[c] - f1[c], 7, 0)
            m1 = jnp.where(sub == 0, x[c] + xf[c], m1)
            p1 = jnp.where(sub == 7, x[c] - xf[c], p1)
            acc = oc[c, i] + CC * q[c] + m1 + p1
            base = BC * q[c]
            p3, m3 = base - AC * f3[c], base + AC * f3[c]
            a, bb = pltpu.roll(p3[:, :128], 127, 1), pltpu.roll(p3[:, 128:], 127, 1)
            e, f = pltpu.roll(m3[:, :128], 1, 1), pltpu.roll(m3[:, 128:], 1, 1)
            lg = pltpu.roll(gl[c], 129 - i, 1) if i > 1 else gl[c]
            rg = pltpu.roll(gr[c], 64 - i, 1)
            lo = jnp.where(last, bb, a) + jnp.where(first, lg, e)
            hi = jnp.where(lane8 == 63, rg, bb) + jnp.where(first, e, f)
            acc = acc + jnp.concatenate([lo, hi], axis=1)
            p2, m2 = base - AC * f2[c], base + AC * f2[c]
            if i > 1:
                done = BX * (oc[c, i - 1] + p2)
                cres[c, i - 2, :, 0:128] = done[:, 0:128]
                cres[c, i - 2, :, 128:192] = done[:, 128:192]
            oc[c, i] = acc
            if i < ROWS:
                oc[c, i + 1] = m2
    q = [cv[c, ROWS + 1, :, :] for c in range(5)]
    f2 = fluxes(q)[2]
    for c in range(5):
        done = BX * (oc[c, ROWS] + BC * q[c] - AC * f2[c])
        cres[c, ROWS - 1, :, 0:128] = done[:, 0:128]
        cres[c, ROWS - 1, :, 128:192] = done[:, 128:192]

    def await_share(d, _):
        @pl.when(d != me)
        def _():
            remote(shs.at[d], shr.at[d], sh_s.at[d], sh_r.at[d], {"azim": d}).wait_recv()

        return 0

    lax.fori_loop(0, NA, await_share, 0)
    cart = [functools.reduce(jnp.add, [shr[d, c] for d in range(NA)]) for c in range(5)]
    g = [cart[0], cart[1], cart[3] * cosine - cart[2] * sine, cart[2] * cosine + cart[3] * sine, cart[4]]
    f3 = fluxes(g)[3]
    for c in range(5):
        xm[8 * c : 8 * c + 8, :] = BR * g[c] + INNER * f3[c]
    fix[...] = xm[...].T
    for c in azim + axial:
        c.wait_recv()

    for c in axial + azim + caxial:
        c.wait_send()

    @pl.when(me > 0)
    def _():
        crow_dn.wait_send()

    @pl.when(me < NA - 1)
    def _():
        crow_up.wait_send()

    for a in range(NA):
        others = [s for s in needed(a) if s != a]

        @pl.when(is_in(me, others))
        def _(a=a):
            tr_copy(a).wait_send()

    def drain(d, _):
        @pl.when(d != me)
        def _():
            sh_copy(d).wait_send()

        return 0

    lax.fori_loop(0, NA, drain, 0)


def closing(ov, hal, ah, fix, core, tab, cyc_out, cor_out, buf, sems):
    core_copy = pltpu.make_async_copy(core, cor_out, sems.at[PL])
    core_copy.start()
    top = lax.broadcasted_iota(jnp.int32, (8, NR), 0) == 0
    bottom = lax.broadcasted_iota(jnp.int32, (8, NR), 0) == 7
    first = lax.broadcasted_iota(jnp.int32, (W, 128), 1) == 0
    ka = jnp.broadcast_to(tab[0:1, :], (8, NR))
    ba = jnp.broadcast_to(tab[1:2, :], (8, NR))

    def copy(p):
        return pltpu.make_async_copy(buf.at[:, p], cyc_out.at[:, p], sems.at[p])

    def plane(p, axial):
        side = [ah[c, p, :, :] for c in range(5)]
        f2 = fluxes(side)[2]
        lo = [jnp.where(top, ba * side[c] + ka * f2[c], 0.0) for c in range(5)]
        hi = [jnp.where(bottom, ba * side[c] - ka * f2[c], 0.0) for c in range(5)]
        for b in range(SEC // W):
            rows = slice(W * b, W * b + W)
            if axial is not None:
                q = [hal[c, axial, rows, :] for c in range(5)]
                f1 = fluxes(q)[1]
            inner = fix[rows, :]
            for c in range(5):
                v = ov[c, p + 1, W * b + W : W * b + 2 * W, :]
                if axial == 0:
                    v = v + (q[c] + f1[c])
                if axial == 1:
                    v = v + (q[c] - f1[c])
                if b == 0:
                    v = jnp.concatenate([v[:8] + lo[c], v[8:]], axis=0)
                if b == SEC // W - 1:
                    v = jnp.concatenate([v[: W - 8], v[W - 8 :] + hi[c]], axis=0)
                col = jnp.where(first, pltpu.roll(inner, lax.rem(128 - 8 * c - p, 128), 1), 0.0)
                buf[c, p, rows, 0:128] = BX * (v[:, :128] + col)
                buf[c, p, rows, 128:256] = BX * v[:, 128:]
        copy(p).start()

    def middle(p, _):
        plane(p, None)
        return 0

    lax.fori_loop(1, PL - 1, middle, 0)
    plane(jnp.int32(0), 0)
    plane(jnp.int32(PL - 1), 1)
    core_copy.wait()
    for p in range(PL):
        copy(p).wait()


def body(cycle_state, core_state, core_taps, core_weights, cycle_taps, cycle_weights):
    tab, trig = tables()
    f32, i32 = jnp.float32, jnp.int32
    dma = pltpu.SemaphoreType.DMA
    core_t = jnp.transpose(core_state, (0, 2, 1, 3))
    hbm = pl.BlockSpec(memory_space=pltpu.HBM)
    vmem = pl.BlockSpec(memory_space=pltpu.VMEM)
    vm = pltpu.VMEM
    shape = lambda *dims: jax.ShapeDtypeStruct(dims, f32)
    operands = [
        pltpu.with_memory_space_constraint(x, pltpu.HBM)
        for x in (
            cycle_state, core_t, core_taps.T, core_weights.T, cycle_taps.T, cycle_weights.T,
            jnp.asarray(tab), jnp.asarray(trig),
        )
    ]
    parts = pl.pallas_call(
        kernel,
        out_shape=(
            shape(5, PL + 2, SEC + W, NR),
            shape(5, 2, SEC, NR),
            shape(5, PL, 8, NR),
            shape(128, 128),
            shape(5, ROWS, PL, NC),
            shape(8, NR),
        ),
        in_specs=[hbm] * 8,
        out_specs=(vmem,) * 6,
        scratch_shapes=[
            vm((5, PL, SEC, NR), f32),
            vm((5, 2, SEC + 4 * W, 128), f32),
            vm((5, 2, SEC + 4 * W, 128), f32),
            vm((5, ROWS, PL, NC), f32),
            vm((5, ROWS + 2, PL, 256), f32),
            vm((5, ROWS + 2, PL, 256), f32),
            vm((5, ROWS, PL, NC), f32),
            vm((5, PL, NC), f32),
            vm((5, PL, NC), f32),
            vm((5, 8, 128), f32),
            vm((NA, 5, 8, 128), f32),
            vm((NA, 5, 8, 128), f32),
            vm((NA, 5, 8, 128), f32),
            vm((128, 128), f32),
            vm((5, 7, 8, 128), f32),
            vm((5, 8, 128), f32),
            vm((5, 8, 128), f32),
            vm((8, NT), f32),
            vm((4, 768), i32),
            vm((4, 768), f32),
            vm((4, NT), i32),
            vm((4, NT), f32),
            pltpu.SemaphoreType.REGULAR,
            dma((PL,)),
            dma((7,)),
            dma((2,)), dma((2,)), dma((2,)), dma((2,)), dma((2,)), dma((2,)), dma((2,)), dma((2,)),
            dma((NA,)), dma((NA,)), dma((NA,)), dma((NA,)),
        ],
        compiler_params=pltpu.CompilerParams(
            collective_id=0, has_side_effects=True, vmem_limit_bytes=24 * 2**20
        ),
    )(*operands)
    cycle_new, core_new = pl.pallas_call(
        closing,
        out_shape=(
            jax.ShapeDtypeStruct(cycle_state.shape, f32),
            jax.ShapeDtypeStruct(core_t.shape, f32),
        ),
        in_specs=[vmem] * 6,
        out_specs=(hbm, hbm),
        scratch_shapes=[vm((5, PL, SEC, NR), f32), dma((PL + 1,))],
        compiler_params=pltpu.CompilerParams(vmem_limit_bytes=12 * 2**20),
    )(*parts)
    return cycle_new, jnp.transpose(core_new, (0, 2, 1, 3))


def solution(mesh):
    placed = (P(None, "axial", "azim", None), P(None, "axial", "azim", None), P(), P(), P(), P())
    return jax.shard_map(
        body,
        mesh=mesh,
        in_specs=placed,
        out_specs=(P(None, "axial", "azim", None), P(None, "axial", "azim", None)),
        check_vma=False,
    )
```

```python
import functools
import math

import jax
import jax.numpy as jnp
import numpy as np
from jax import lax
from jax.experimental import pallas as pl
from jax.experimental.pallas import tpu as pltpu
from jax.sharding import PartitionSpec as P

DT = 0.001
DX = 0.004
DR = 1.0 / 256.0
DC = 2.0 / 192.0
NU = 0.002
NT = 2048
NR = 256
NC = 192
PL = 8
SEC = 128
ROWS = 12
W = 16
NA = 16
HUB = NA - 1
DA = 2.0 * math.pi / NT

BX = NU * DT / DX**2
AX = DT / (2.0 * DX)
BR = NU * DT / DR**2 / BX
AC = DT / (2.0 * DC) / BX
BC = NU * DT / DC**2 / BX
SX = DX / (2.0 * NU)


def tables():
    radius = lambda i: 1.0 + (i + 0.5) / 256.0
    i = np.arange(NR, dtype=np.float64)
    tab = np.zeros((8, NR))
    tab[0] = DT / (2.0 * DA * radius(i)) / BX
    tab[1] = NU * DT / (DA * radius(i)) ** 2 / BX
    tab[2] = DT * radius(i) / (2.0 * DR * radius(i - 1)) / BX
    tab[3] = DT * radius(i) / (2.0 * DR * radius(i + 1)) / BX
    tab[3, -1] = DT * radius(NR) / (2.0 * DR * radius(NR - 1)) / BX
    tab[4] = 1.0 / BX - 2.0 - 2.0 * BR - 2.0 * tab[1]
    tab[5] = DT / radius(i) / BX
    angle = (np.arange(NT) + 0.5) * (2.0 * math.pi / NT)
    trig = np.zeros((8, NT))
    trig[0] = np.cos(angle)
    trig[1] = np.sin(angle)
    return tab.astype(np.float32), trig.astype(np.float32)


INNER = float(DT * (1.0 - 0.5 / 256.0) / (2.0 * DR * (1.0 + 0.5 / 256.0)) / BX)
CC = float(1.0 / BX - 2.0 - 4.0 * BC)


def needed(a):
    spans = [(32 * a - 8, 32 * a + 37), (32 * a + 504, 32 * a + 549)]
    if a == 0:
        spans.append((1016, 1541))
    if a == NA - 1:
        spans.append((1528, 2053))
    full, edge = set(), set()
    for lo, hi in spans:
        for s in range(lo // SEC, hi // SEC + 1):
            start, stop = max(lo - s * SEC, 0), min(hi - s * SEC, SEC - 1)
            (edge if stop < 8 or start >= SEC - 8 else full).add(s % NA)
    return sorted(full - {a}), sorted(edge - full - {a})


def fluxes(q):
    inv = pltpu.reciprocal(q[0], approx=False)
    u1, u2, u3 = q[1] * inv, q[2] * inv, q[3] * inv
    p11, p22, p33 = q[1] * u1, q[2] * u2, q[3] * u3
    p12, p13, p23 = q[1] * u2, q[1] * u3, q[2] * u3
    pr = 0.4 * q[4] - 0.2 * (p11 + p22 + p33)
    h = q[4] + pr
    return (
        None,
        [q[1], p11 + pr, p12, p13, h * u1],
        [q[2], p12, p22 + pr, p23, h * u2],
        [q[3], p13, p23, p33 + pr, h * u3],
    )


def kernel(
    cyc, cor, ctaps, cwts, ytaps, ywts, tab_in, trig_in, ov, hal, ah, fix, cres, tab,
    qv, p2s, m2s, cin, cv, oc, chx, crlo, crhi, trs, tre, trr, shs, shr, xm, ep, gl, gr, trig, ct, cw, yt, yw,
    all_in, in_sem, sm_sem, ax_s, ax_r, cx_s, cx_r, ar_s, ar_r, cr_s, cr_r, tr_s, tr_r, sh_s, sh_r,
):
    me = lax.axis_index("azim")
    ax = lax.axis_index("axial")
    n_ax = lax.axis_size("axial")
    up_ax = {"axial": lax.rem(ax + 1, n_ax)}
    dn_ax = {"axial": lax.rem(ax + n_ax - 1, n_ax)}
    up_az = {"azim": lax.rem(me + 1, NA)}
    dn_az = {"azim": lax.rem(me + NA - 1, NA)}
    MESH = pl.DeviceIdType.MESH

    barrier = pltpu.get_barrier_semaphore()
    pl.semaphore_signal(barrier, inc=1, device_id=up_ax, device_id_type=MESH)
    pl.semaphore_signal(barrier, inc=1, device_id=dn_ax, device_id_type=MESH)

    @pl.when(jnp.logical_and(me != HUB, me != 0))
    def _():
        pl.semaphore_signal(barrier, inc=1, device_id={"azim": HUB}, device_id_type=MESH)

    def greet(d, _):
        pl.semaphore_signal(barrier, inc=1, device_id={"azim": d}, device_id_type=MESH)
        return 0

    lax.fori_loop(1, jnp.where(me == 0, NA, 1), greet, 0)

    smalls = [
        pltpu.make_async_copy(s, d, sm_sem.at[i])
        for i, (s, d) in enumerate(
            [(cor, cin), (ytaps, yt), (ywts, yw), (tab_in, tab), (trig_in, trig), (ctaps, ct), (cwts, cw)]
        )
    ]
    planes = [pltpu.make_async_copy(cyc.at[:, p], qv.at[:, p], in_sem.at[p]) for p in range(PL)]
    for c in smalls:
        c.start()
    for c in planes:
        c.start()

    def remote(src, dst, s, r, dev):
        return pltpu.make_async_remote_copy(
            src_ref=src, dst_ref=dst, send_sem=s, recv_sem=r, device_id=dev, device_id_type=MESH
        )

    axial = [
        remote(cyc.at[:, 0], hal.at[:, 1], ax_s.at[0], ax_r.at[0], dn_ax),
        remote(cyc.at[:, PL - 1], hal.at[:, 0], ax_s.at[1], ax_r.at[1], up_ax),
    ]
    caxial = [
        remote(cor.at[:, :, 0, :], chx.at[:, :, PL - 1, :], cx_s.at[0], cx_r.at[0], dn_ax),
        remote(cor.at[:, :, PL - 1, :], chx.at[:, :, 0, :], cx_s.at[1], cx_r.at[1], up_ax),
    ]
    azim = [
        remote(cyc.at[:, :, 0, :], ah.at[:, :, 7, :], ar_s.at[0], ar_r.at[0], dn_az),
        remote(cyc.at[:, :, SEC - 1, :], ah.at[:, :, 0, :], ar_s.at[1], ar_r.at[1], up_az),
    ]
    crow_dn = remote(cor.at[:, 0], crhi, cr_s.at[0], cr_r.at[0], dn_az)
    crow_up = remote(cor.at[:, ROWS - 1], crlo, cr_s.at[1], cr_r.at[1], up_az)

    lane8 = lax.broadcasted_iota(jnp.int32, (8, 128), 1)
    row8 = lax.broadcasted_iota(jnp.int32, (8, 128), 0)

    def prepare():
        for c in smalls:
            c.wait()
        for i in range(ROWS):
            for c in range(5):
                cv[c, i + 1, :, 0:128] = cin[c, i, :, 0:128]
                cv[c, i + 1, :, 128:192] = cin[c, i, :, 128:192]

        for c in range(5):
            v = jnp.zeros((8, 128), jnp.float32)
            for i in range(ROWS):
                left = pltpu.roll(cv[c, i + 1, :, 0:128], 8 * i, 1)
                right = pltpu.roll(cv[c, i + 1, :, 128:256], (8 * i + 4 - 60) % 128, 1)
                v = jnp.where((lane8 >> 3) == i, jnp.where((lane8 & 7) < 4, left, right), v)
            ep[c, 6] = v

    @pl.when(ax < 2)
    def _():
        prepare()

    pl.semaphore_wait(barrier, 2 + jnp.where(me == HUB, NA - 1, jnp.where(me == 0, 0, 1)))
    for c in axial + caxial:
        c.start()

    def tell(d, _):
        pl.semaphore_signal(all_in, inc=1, device_id={"azim": d}, device_id_type=MESH)
        return 0

    lax.fori_loop(0, jnp.where(me == HUB, NA - 1, 0), tell, 0)

    @pl.when(ax >= 2)
    def _():
        prepare()

    def bcast(x):
        return jnp.broadcast_to(x, (8, 128))

    def tap_cells(d):
        cols = pl.ds(pl.multiple_of(d * SEC, SEC), SEC)
        ws = [yw[k : k + 1, cols] for k in range(4)]
        total = ws[0] + ws[1] + ws[2] + ws[3]
        cells = []
        for k in range(4):
            tap = bcast(yt[k : k + 1, cols])
            row = ((tap >> 6) * 43691) >> 17
            cells.append((row - me * ROWS, tap - row * NC, bcast(ws[k] / total)))
        return cells

    def share(d, _):
        acc = [jnp.zeros((8, 128), jnp.float32) for _ in range(5)]
        for lrow, col, w in tap_cells(d):
            inside = jnp.logical_and(lrow >= 0, lrow < ROWS)
            side = jnp.logical_or(col < 4, col >= NC - 4)
            idx = (lrow * 8 + jnp.where(col < 4, col, col - (NC - 8))) & 127
            wk = jnp.where(jnp.logical_and(inside, side), w, 0.0)
            for c in range(5):
                acc[c] = acc[c] + wk * jnp.take_along_axis(ep[c, 6], idx, axis=1)
        for c in range(5):
            shs[d, c] = acc[c]
        return 0

    lax.fori_loop(0, NA, share, 0, unroll=4)

    r0 = jnp.where(me == 0, 0, ROWS - 4)

    @pl.when(jnp.logical_or(me == 0, me == NA - 1))
    def _():
        for c in range(5):
            for r in range(4):
                ep[c, r] = cv[c, r0 + r + 1, :, 0:128]
            for j in range(2):
                even = cv[c, r0 + 2 * j + 1, :, 128:256]
                odd = cv[c, r0 + 2 * j + 2, :, 128:256]
                ep[c, 4 + j] = jnp.where(lane8 < 64, even, pltpu.roll(odd, 64, 1))

    def outer(d, _):
        acc = [shs[d, c] for c in range(5)]
        for lrow, col, w in tap_cells(d):
            r = lrow - r0
            mid = jnp.logical_and(col >= 4, col < NC - 4)
            ok = jnp.logical_and(mid, jnp.logical_and(r >= 0, r < 4))
            wk = jnp.where(ok, w, 0.0)
            high = col >= 128
            group = jnp.where(high, 4 + (r >> 1), r)
            idx = jnp.where(high, (col & 63) + ((r & 1) << 6), col) & 127
            for s in range(6):
                ws = jnp.where(group == s, wk, 0.0)
                for c in range(5):
                    acc[c] = acc[c] + ws * jnp.take_along_axis(ep[c, s], idx, axis=1)
        for c in range(5):
            shs[d, c] = acc[c]
        return 0


    def sh_copy(d):
        return remote(shs.at[d], shr.at[me], sh_s.at[d], sh_r.at[me], {"azim": d})

    def send_share(d, _):
        @pl.when(d != me)
        def _():
            sh_copy(d).start()

        return 0

    def outer_and_send(d, _):
        outer(d, 0)
        return send_share(d, 0)

    lane_s = lax.broadcasted_iota(jnp.int32, (SEC, 128), 1)
    own = pl.ds(pl.multiple_of(me * SEC, SEC), SEC)
    cosine = jnp.broadcast_to(trig[0:1, own], (8, 128))
    sine = jnp.broadcast_to(trig[1:2, own], (8, 128))

    def trace():
        for c in planes:
            c.wait()
        tt = jnp.zeros((SEC, 128), jnp.float32)
        for p in range(PL):
            for c in range(5):
                ch = c * 8 + p
                x = qv[c, p, :, 0:128]
                tt = jnp.where(lane_s == ch, pltpu.roll(x, ch, 1) if ch else x, tt)
        tt = tt.T
        tq = [tt[8 * c : 8 * c + 8, :] for c in range(5)]
        cart = [tq[0], tq[1], tq[3] * cosine - tq[2] * sine, tq[3] * sine + tq[2] * cosine, tq[4]]
        ends = jnp.zeros((8, 128), jnp.float32)
        for c in range(5):
            trs[c] = cart[c]
            trr[me, c] = cart[c]
            head = pltpu.roll(cart[c], 16 * c, 1) if c else cart[c]
            tail = pltpu.roll(cart[c], (16 * c + 16) % 128, 1)
            ends = jnp.where((lane8 >> 4) == c, jnp.where((lane8 & 15) < 8, head, tail), ends)
        trs[5] = ends

    first, last = lane8 == 0, lane8 == 127
    zero8 = jnp.zeros((8, 128), jnp.float32)
    wide_first = lax.broadcasted_iota(jnp.int32, (W, 128), 1) == 0
    wide_last = lax.broadcasted_iota(jnp.int32, (W, 128), 1) == 127
    for c in range(5):
        for h in range(2):
            m2s[c, h, 2 * W - 8 : 2 * W, :] = zero8
            p2s[c, h, 2 * W + SEC : 2 * W + SEC + 8, :] = zero8
        ov[c, 1, W : W + SEC, :] = jnp.zeros((SEC, NR), jnp.float32)

    def cycle_plane(p, _):
        for b in range(SEC // W + 1):
            rows, prev, now = pl.ds(W * b + W, W), pl.ds(W * b, W), pl.ds(W * b + 2 * W, W)
            if b < SEC // W:
                q = [qv[c, p, W * b : W * b + W, :] for c in range(5)]
                _, f1, f2, f3 = fluxes(q)
                row = lambda k: jnp.broadcast_to(tab[k : k + 1, :], (W, NR))
                ka, ba, cp, cm, cc, so = [row(k) for k in range(6)]
                for c in range(5):
                    ov[c, p, rows, :] += q[c] - f1[c]
                    acc = ov[c, p + 1, rows, :] + cc * q[c]
                    ov[c, p + 2, rows, :] = q[c] + f1[c]
                    base = BR * q[c]
                    p3 = base - cp * f3[c]
                    m3 = base + cm * f3[c]
                    pl0, pl1 = pltpu.roll(p3[:, :128], 127, 1), pltpu.roll(p3[:, 128:], 127, 1)
                    ml0, ml1 = pltpu.roll(m3[:, :128], 1, 1), pltpu.roll(m3[:, 128:], 1, 1)
                    wall = m3[:, 128:] if c != 3 else -m3[:, 128:]
                    lo = jnp.where(wide_last, pl1, pl0) + jnp.where(wide_first, 0.0, ml0)
                    hi = jnp.where(wide_last, wall, pl1) + jnp.where(wide_first, ml0, ml1)
                    acc = acc + jnp.concatenate([lo, hi], axis=1)
                    if c == 2:
                        acc = acc - so * f2[3]
                    if c == 3:
                        acc = acc + so * f2[2]
                    ov[c, p + 1, rows, :] = acc
                    bq, kf = ba * q[c], ka * f2[c]
                    p2, m2 = bq - kf, bq + kf
                    for h in range(2):
                        half = slice(128 * h, 128 * h + 128)
                        p2s[c, h, now, :] = p2[:, half]
                        m2s[c, h, now, :] = m2[:, half]
            if b:
                for c in range(5):
                    for h in range(2):
                        half = slice(128 * h, 128 * h + 128)
                        up = p2s[c, h, pl.ds(W * b + W + 1, W), :]
                        dn = m2s[c, h, pl.ds(W * b + W - 1, W), :]
                        ov[c, p + 1, prev, half] += up + dn
        return 0

    ahead = jnp.where(me == 0, 0, jnp.maximum((12 - me) // 4, 0))
    trace()

    @pl.when(me == 0)
    def _():
        lax.fori_loop(0, NA, outer, 0, unroll=2)

    def tr_copy(d, src, edge):
        if edge:
            return remote(trs.at[5], tre.at[src], tr_s.at[d], tr_r.at[src], {"azim": d})
        return remote(trs.at[0:5], trr.at[src], tr_s.at[d], tr_r.at[src], {"azim": d})

    def is_in(x, items):
        hit = x == items[0]
        for it in items[1:]:
            hit = jnp.logical_or(hit, x == it)
        return hit

    between = jnp.logical_and(me != 0, me != HUB)

    for edge in range(2):

        @pl.when(jnp.logical_and(between, is_in(me, needed(0)[edge])))
        def _(edge=edge):
            tr_copy(0, me, edge).start()

    @pl.when(between)
    def _():
        sh_copy(0).start()

    lax.fori_loop(0, ahead, cycle_plane, 0)

    @pl.when(me != HUB)
    def _():
        pl.semaphore_wait(all_in, 1)

    for a in range(NA):
        for edge in range(2):
            givers = [s for s in needed(a)[edge] if a or s == HUB]
            if givers:

                @pl.when(is_in(me, givers))
                def _(a=a, edge=edge):
                    tr_copy(a, me, edge).start()

    for c in azim:
        c.start()

    @pl.when(me > 0)
    def _():
        crow_dn.start()

    @pl.when(me < NA - 1)
    def _():
        crow_up.start()

    @pl.when(me == NA - 1)
    def _():
        lax.fori_loop(0, NA, outer_and_send, 0)

    @pl.when(me != NA - 1)
    def _():
        lax.fori_loop(1, NA, send_share, 0)

    for c in range(5):
        shr[me, c] = shs[me, c]

    lax.fori_loop(ahead, PL, cycle_plane, 0)

    for s in range(NA):
        for edge in range(2):
            takers = [a for a in range(NA) if s in needed(a)[edge]]
            if takers:

                @pl.when(is_in(me, takers))
                def _(s=s, edge=edge):
                    tr_copy(s, s, edge).wait_recv()
                    if edge:
                        for c in range(5):
                            ends = tre[s]
                            head = pltpu.roll(ends, 128 - 16 * c, 1) if c else ends
                            tail = pltpu.roll(ends, 112 - 16 * c, 1)
                            trr[s, c] = jnp.where(lane8 < 8, head, tail)

    s0 = ((32 * me + 2040) >> 7) & 15
    s1 = ((32 * me + 37) >> 7) & 15

    def ghost(start, shift, sectors):
        vals = [zero8 for _ in range(5)]
        ws = [bcast_roll(cw[k : k + 1, start : start + 256], shift) for k in range(4)]
        total = ws[0] + ws[1] + ws[2] + ws[3]
        for k in range(4):
            tap = bcast_roll(ct[k : k + 1, start : start + 256], shift)
            idx = tap & 127
            sec = tap >> 7
            w = ws[k] / total
            for c in range(5):
                v = jnp.take_along_axis(trr[sectors[0], c], idx, axis=1)
                for s in sectors[1:]:
                    v = jnp.where(sec == s, jnp.take_along_axis(trr[s, c], idx, axis=1), v)
                vals[c] = vals[c] + w * v
        return vals

    def bcast_roll(x, shift):
        full = jnp.broadcast_to(x, (8, 256))
        if isinstance(shift, int):
            return (pltpu.roll(full, 256 - shift, 1) if shift else full)[:, :128]
        return pltpu.roll(full, shift, 1)[:, :128]

    def col_terms(g):
        return fluxes(g)[3]

    back = lax.rem(512 - ROWS * me, 256)
    g = ghost(0, back, [s0, s1])
    f = col_terms(g)
    for c in range(5):
        gl[c] = BC * g[c] + AC * f[c]
    back = lax.rem(512 - 64 - ROWS * me, 256)
    g = ghost(128, back, [(s0 + 4) & 15, (s1 + 4) & 15])
    f = col_terms(g)
    for c in range(5):
        gr[c] = BC * g[c] - AC * f[c]

    @pl.when(me > 0)
    def _():
        crow_up.wait_recv()
        for c in range(5):
            cv[c, 0, :, 0:128] = crlo[c, :, 0:128]
            cv[c, 0, :, 128:192] = crlo[c, :, 128:192]

    @pl.when(me < NA - 1)
    def _():
        crow_dn.wait_recv()
        for c in range(5):
            cv[c, ROWS + 1, :, 0:128] = crhi[c, :, 0:128]
            cv[c, ROWS + 1, :, 128:192] = crhi[c, :, 128:192]

    @pl.when(me == 0)
    def _():
        for h in range(2):
            g = ghost(384, 0, list(range(7, 13))) if h == 0 else ghost(384, 128, list(range(7, 13)))
            for c in range(5):
                cv[c, 0, :, 128 * h : 128 * h + 128] = g[c]

    @pl.when(me == NA - 1)
    def _():
        g = ghost(512, 64, [11, 12, 13, 14, 15, 0])
        for c in range(5):
            cv[c, ROWS + 1, :, 0:128] = g[c]
        g = ghost(512, 192, [11, 12, 13, 14, 15, 0])
        for c in range(5):
            cv[c, ROWS + 1, :, 128:256] = g[c]

    for c in caxial:
        c.wait_recv()

    sub = lax.broadcasted_iota(jnp.int32, (8, 256), 0)
    q = [cv[c, 0, :, :] for c in range(5)]
    f2 = fluxes(q)[2]
    for c in range(5):
        oc[c, 1] = BC * q[c] + AC * f2[c]
    for i in range(1, ROWS + 1):
        q = [cv[c, i, :, :] for c in range(5)]
        _, f1, f2, f3 = fluxes(q)
        x = [chx[c, i - 1, :, :] for c in range(5)]
        x = [jnp.concatenate([v, jnp.ones((8, 64), jnp.float32)], axis=1) for v in x]
        xf = fluxes(x)[1]
        for c in range(5):
            m1 = pltpu.roll(q[c] + f1[c], 1, 0)
            p1 = pltpu.roll(q[c] - f1[c], 7, 0)
            m1 = jnp.where(sub == 0, x[c] + xf[c], m1)
            p1 = jnp.where(sub == 7, x[c] - xf[c], p1)
            acc = oc[c, i] + CC * q[c] + m1 + p1
            base = BC * q[c]
            p3, m3 = base - AC * f3[c], base + AC * f3[c]
            a, bb = pltpu.roll(p3[:, :128], 127, 1), pltpu.roll(p3[:, 128:], 127, 1)
            e, f = pltpu.roll(m3[:, :128], 1, 1), pltpu.roll(m3[:, 128:], 1, 1)
            lg = pltpu.roll(gl[c], 129 - i, 1) if i > 1 else gl[c]
            rg = pltpu.roll(gr[c], 64 - i, 1)
            lo = jnp.where(last, bb, a) + jnp.where(first, lg, e)
            hi = jnp.where(lane8 == 63, rg, bb) + jnp.where(first, e, f)
            acc = acc + jnp.concatenate([lo, hi], axis=1)
            p2, m2 = base - AC * f2[c], base + AC * f2[c]
            if i > 1:
                done = BX * (oc[c, i - 1] + p2)
                cres[c, i - 2, :, 0:128] = done[:, 0:128]
                cres[c, i - 2, :, 128:192] = done[:, 128:192]
            oc[c, i] = acc
            if i < ROWS:
                oc[c, i + 1] = m2
    q = [cv[c, ROWS + 1, :, :] for c in range(5)]
    f2 = fluxes(q)[2]
    for c in range(5):
        done = BX * (oc[c, ROWS] + BC * q[c] - AC * f2[c])
        cres[c, ROWS - 1, :, 0:128] = done[:, 0:128]
        cres[c, ROWS - 1, :, 128:192] = done[:, 128:192]

    def await_share(d, _):
        @pl.when(d != me)
        def _():
            remote(shs.at[d], shr.at[d], sh_s.at[d], sh_r.at[d], {"azim": d}).wait_recv()

        return 0

    lax.fori_loop(0, NA, await_share, 0)
    cart = [functools.reduce(jnp.add, [shr[d, c] for d in range(NA)]) for c in range(5)]
    g = [cart[0], cart[1], cart[3] * cosine - cart[2] * sine, cart[2] * cosine + cart[3] * sine, cart[4]]
    f3 = fluxes(g)[3]
    for c in range(5):
        xm[8 * c : 8 * c + 8, :] = BR * g[c] + INNER * f3[c]
    fix[...] = xm[...].T
    for c in azim + axial:
        c.wait_recv()

    for c in axial + azim + caxial:
        c.wait_send()

    @pl.when(me > 0)
    def _():
        crow_dn.wait_send()

    @pl.when(me < NA - 1)
    def _():
        crow_up.wait_send()

    for a in range(NA):
        for edge in range(2):
            givers = needed(a)[edge]
            if givers:

                @pl.when(is_in(me, givers))
                def _(a=a, edge=edge):
                    tr_copy(a, me, edge).wait_send()

    def drain(d, _):
        @pl.when(d != me)
        def _():
            sh_copy(d).wait_send()

        return 0

    lax.fori_loop(0, NA, drain, 0)


def closing(ov, hal, ah, fix, core, tab, cyc_out, cor_out, buf, sems):
    core_copy = pltpu.make_async_copy(core, cor_out, sems.at[PL])
    core_copy.start()
    top = lax.broadcasted_iota(jnp.int32, (8, NR), 0) == 0
    bottom = lax.broadcasted_iota(jnp.int32, (8, NR), 0) == 7
    first = lax.broadcasted_iota(jnp.int32, (W, 128), 1) == 0
    ka = jnp.broadcast_to(tab[0:1, :], (8, NR))
    ba = jnp.broadcast_to(tab[1:2, :], (8, NR))

    def copy(p):
        return pltpu.make_async_copy(buf.at[:, p], cyc_out.at[:, p], sems.at[p])

    def plane(p, axial):
        side = [ah[c, p, :, :] for c in range(5)]
        f2 = fluxes(side)[2]
        lo = [jnp.where(top, ba * side[c] + ka * f2[c], 0.0) for c in range(5)]
        hi = [jnp.where(bottom, ba * side[c] - ka * f2[c], 0.0) for c in range(5)]
        for b in range(SEC // W):
            rows = slice(W * b, W * b + W)
            if axial is not None:
                q = [hal[c, axial, rows, :] for c in range(5)]
                f1 = fluxes(q)[1]
            inner = fix[rows, :]
            for c in range(5):
                v = ov[c, p + 1, W * b + W : W * b + 2 * W, :]
                if axial == 0:
                    v = v + (q[c] + f1[c])
                if axial == 1:
                    v = v + (q[c] - f1[c])
                if b == 0:
                    v = jnp.concatenate([v[:8] + lo[c], v[8:]], axis=0)
                if b == SEC // W - 1:
                    v = jnp.concatenate([v[: W - 8], v[W - 8 :] + hi[c]], axis=0)
                col = jnp.where(first, pltpu.roll(inner, lax.rem(128 - 8 * c - p, 128), 1), 0.0)
                buf[c, p, rows, 0:128] = BX * (v[:, :128] + col)
                buf[c, p, rows, 128:256] = BX * v[:, 128:]
        copy(p).start()

    def middle(p, _):
        plane(p, None)
        return 0

    lax.fori_loop(1, PL - 1, middle, 0)
    plane(jnp.int32(0), 0)
    plane(jnp.int32(PL - 1), 1)
    core_copy.wait()
    for p in range(PL):
        copy(p).wait()


def body(cycle_state, core_state, core_taps, core_weights, cycle_taps, cycle_weights):
    tab, trig = tables()
    f32, i32 = jnp.float32, jnp.int32
    dma = pltpu.SemaphoreType.DMA
    core_t = jnp.transpose(core_state, (0, 2, 1, 3))
    hbm = pl.BlockSpec(memory_space=pltpu.HBM)
    vmem = pl.BlockSpec(memory_space=pltpu.VMEM)
    vm = pltpu.VMEM
    shape = lambda *dims: jax.ShapeDtypeStruct(dims, f32)
    operands = [
        pltpu.with_memory_space_constraint(x, pltpu.HBM)
        for x in (
            cycle_state, core_t, core_taps.T, core_weights.T, cycle_taps.T, cycle_weights.T,
            jnp.asarray(tab), jnp.asarray(trig),
        )
    ]
    parts = pl.pallas_call(
        kernel,
        out_shape=(
            shape(5, PL + 2, SEC + W, NR),
            shape(5, 2, SEC, NR),
            shape(5, PL, 8, NR),
            shape(128, 128),
            shape(5, ROWS, PL, NC),
            shape(8, NR),
        ),
        in_specs=[hbm] * 8,
        out_specs=(vmem,) * 6,
        scratch_shapes=[
            vm((5, PL, SEC, NR), f32),
            vm((5, 2, SEC + 4 * W, 128), f32),
            vm((5, 2, SEC + 4 * W, 128), f32),
            vm((5, ROWS, PL, NC), f32),
            vm((5, ROWS + 2, PL, 256), f32),
            vm((5, ROWS + 2, PL, 256), f32),
            vm((5, ROWS, PL, NC), f32),
            vm((5, PL, NC), f32),
            vm((5, PL, NC), f32),
            vm((6, 8, 128), f32),
            vm((NA, 8, 128), f32),
            vm((NA, 5, 8, 128), f32),
            vm((NA, 5, 8, 128), f32),
            vm((NA, 5, 8, 128), f32),
            vm((128, 128), f32),
            vm((5, 7, 8, 128), f32),
            vm((5, 8, 128), f32),
            vm((5, 8, 128), f32),
            vm((8, NT), f32),
            vm((4, 768), i32),
            vm((4, 768), f32),
            vm((4, NT), i32),
            vm((4, NT), f32),
            pltpu.SemaphoreType.REGULAR,
            dma((PL,)),
            dma((7,)),
            dma((2,)), dma((2,)), dma((2,)), dma((2,)), dma((2,)), dma((2,)), dma((2,)), dma((2,)),
            dma((NA,)), dma((NA,)), dma((NA,)), dma((NA,)),
        ],
        compiler_params=pltpu.CompilerParams(
            collective_id=0, has_side_effects=True, vmem_limit_bytes=24 * 2**20
        ),
    )(*operands)
    cycle_new, core_new = pl.pallas_call(
        closing,
        out_shape=(
            jax.ShapeDtypeStruct(cycle_state.shape, f32),
            jax.ShapeDtypeStruct(core_t.shape, f32),
        ),
        in_specs=[vmem] * 6,
        out_specs=(hbm, hbm),
        scratch_shapes=[vm((5, PL, SEC, NR), f32), dma((PL + 1,))],
        compiler_params=pltpu.CompilerParams(vmem_limit_bytes=12 * 2**20),
    )(*parts)
    return cycle_new, jnp.transpose(core_new, (0, 2, 1, 3))


def solution(mesh):
    placed = (P(None, "axial", "azim", None), P(None, "axial", "azim", None), P(), P(), P(), P())
    return jax.shard_map(
        body,
        mesh=mesh,
        in_specs=placed,
        out_specs=(P(None, "axial", "azim", None), P(None, "axial", "azim", None)),
        check_vma=False,
    )
```

```python
import functools
import math

import jax
import jax.numpy as jnp
import numpy as np
from jax import lax
from jax.experimental import pallas as pl
from jax.experimental.pallas import tpu as pltpu
from jax.sharding import PartitionSpec as P

DT = 0.001
DX = 0.004
DR = 1.0 / 256.0
DC = 2.0 / 192.0
NU = 0.002
NT = 2048
NR = 256
NC = 192
PL = 8
SEC = 128
ROWS = 12
W = 16
NA = 16
HUB = NA - 1
DA = 2.0 * math.pi / NT

BX = NU * DT / DX**2
AX = DT / (2.0 * DX)
BR = NU * DT / DR**2 / BX
AC = DT / (2.0 * DC) / BX
BC = NU * DT / DC**2 / BX
SX = DX / (2.0 * NU)


def tables():
    radius = lambda i: 1.0 + (i + 0.5) / 256.0
    i = np.arange(NR, dtype=np.float64)
    tab = np.zeros((8, NR))
    tab[0] = DT / (2.0 * DA * radius(i)) / BX
    tab[1] = NU * DT / (DA * radius(i)) ** 2 / BX
    tab[2] = DT * radius(i) / (2.0 * DR * radius(i - 1)) / BX
    tab[3] = DT * radius(i) / (2.0 * DR * radius(i + 1)) / BX
    tab[3, -1] = DT * radius(NR) / (2.0 * DR * radius(NR - 1)) / BX
    tab[4] = 1.0 / BX - 2.0 - 2.0 * BR - 2.0 * tab[1]
    tab[5] = DT / radius(i) / BX
    angle = (np.arange(NT) + 0.5) * (2.0 * math.pi / NT)
    trig = np.zeros((8, NT))
    trig[0] = np.cos(angle)
    trig[1] = np.sin(angle)
    return tab.astype(np.float32), trig.astype(np.float32)


INNER = float(DT * (1.0 - 0.5 / 256.0) / (2.0 * DR * (1.0 + 0.5 / 256.0)) / BX)
CC = float(1.0 / BX - 2.0 - 4.0 * BC)


def needed(a):
    spans = [(32 * a - 8, 32 * a + 37), (32 * a + 504, 32 * a + 549)]
    if a == 0:
        spans.append((1016, 1541))
    if a == NA - 1:
        spans.append((1528, 2053))
    full, edge = set(), set()
    for lo, hi in spans:
        for s in range(lo // SEC, hi // SEC + 1):
            start, stop = max(lo - s * SEC, 0), min(hi - s * SEC, SEC - 1)
            (edge if stop < 8 or start >= SEC - 8 else full).add(s % NA)
    return sorted(full - {a}), sorted(edge - full - {a})


def fluxes(q):
    inv = pltpu.reciprocal(q[0], approx=False)
    u1, u2, u3 = q[1] * inv, q[2] * inv, q[3] * inv
    p11, p22, p33 = q[1] * u1, q[2] * u2, q[3] * u3
    p12, p13, p23 = q[1] * u2, q[1] * u3, q[2] * u3
    pr = 0.4 * q[4] - 0.2 * (p11 + p22 + p33)
    h = q[4] + pr
    return (
        None,
        [q[1], p11 + pr, p12, p13, h * u1],
        [q[2], p12, p22 + pr, p23, h * u2],
        [q[3], p13, p23, p33 + pr, h * u3],
    )


def kernel(
    cyc, cor, ctaps, cwts, ytaps, ywts, tab_in, trig_in, ov, hal, ah, fix, cres, tab,
    qv, p2s, m2s, cin, cv, oc, chx, crlo, crhi, trs, tre, trr, shs, shr, xm, ep, gl, gr, trig, ct, cw, yt, yw,
    all_in, in_sem, sm_sem, ax_s, ax_r, cx_s, cx_r, ar_s, ar_r, cr_s, cr_r, tr_s, tr_r, sh_s, sh_r,
):
    me = lax.axis_index("azim")
    ax = lax.axis_index("axial")
    n_ax = lax.axis_size("axial")
    up_ax = {"axial": lax.rem(ax + 1, n_ax)}
    dn_ax = {"axial": lax.rem(ax + n_ax - 1, n_ax)}
    up_az = {"azim": lax.rem(me + 1, NA)}
    dn_az = {"azim": lax.rem(me + NA - 1, NA)}
    MESH = pl.DeviceIdType.MESH

    barrier = pltpu.get_barrier_semaphore()
    pl.semaphore_signal(barrier, inc=1, device_id=up_ax, device_id_type=MESH)
    pl.semaphore_signal(barrier, inc=1, device_id=dn_ax, device_id_type=MESH)

    @pl.when(jnp.logical_and(me != HUB, me != 0))
    def _():
        pl.semaphore_signal(barrier, inc=1, device_id={"azim": HUB}, device_id_type=MESH)

    def greet(d, _):
        pl.semaphore_signal(barrier, inc=1, device_id={"azim": d}, device_id_type=MESH)
        return 0

    lax.fori_loop(1, jnp.where(me == 0, NA, 1), greet, 0)

    smalls = [
        pltpu.make_async_copy(s, d, sm_sem.at[i])
        for i, (s, d) in enumerate(
            [(cor, cin), (ytaps, yt), (ywts, yw), (tab_in, tab), (trig_in, trig), (ctaps, ct), (cwts, cw)]
        )
    ]
    planes = [pltpu.make_async_copy(cyc.at[:, p], qv.at[:, p], in_sem.at[p]) for p in range(PL)]
    for c in smalls:
        c.start()
    for c in planes:
        c.start()

    def remote(src, dst, s, r, dev):
        return pltpu.make_async_remote_copy(
            src_ref=src, dst_ref=dst, send_sem=s, recv_sem=r, device_id=dev, device_id_type=MESH
        )

    axial = [
        remote(cyc.at[:, 0], hal.at[:, 1], ax_s.at[0], ax_r.at[0], dn_ax),
        remote(cyc.at[:, PL - 1], hal.at[:, 0], ax_s.at[1], ax_r.at[1], up_ax),
    ]
    caxial = [
        remote(cor.at[:, :, 0, :], chx.at[:, :, PL - 1, :], cx_s.at[0], cx_r.at[0], dn_ax),
        remote(cor.at[:, :, PL - 1, :], chx.at[:, :, 0, :], cx_s.at[1], cx_r.at[1], up_ax),
    ]
    azim = [
        remote(cyc.at[:, :, 0, :], ah.at[:, :, 7, :], ar_s.at[0], ar_r.at[0], dn_az),
        remote(cyc.at[:, :, SEC - 1, :], ah.at[:, :, 0, :], ar_s.at[1], ar_r.at[1], up_az),
    ]
    crow_dn = remote(cor.at[:, 0], crhi, cr_s.at[0], cr_r.at[0], dn_az)
    crow_up = remote(cor.at[:, ROWS - 1], crlo, cr_s.at[1], cr_r.at[1], up_az)

    lane8 = lax.broadcasted_iota(jnp.int32, (8, 128), 1)
    row8 = lax.broadcasted_iota(jnp.int32, (8, 128), 0)

    def prepare():
        for c in smalls:
            c.wait()
        for i in range(ROWS):
            for c in range(5):
                cv[c, i + 1, :, 0:128] = cin[c, i, :, 0:128]
                cv[c, i + 1, :, 128:192] = cin[c, i, :, 128:192]

        for c in range(5):
            v = jnp.zeros((8, 128), jnp.float32)
            for i in range(ROWS):
                left = pltpu.roll(cv[c, i + 1, :, 0:128], 8 * i, 1)
                right = pltpu.roll(cv[c, i + 1, :, 128:256], (8 * i + 4 - 60) % 128, 1)
                v = jnp.where((lane8 >> 3) == i, jnp.where((lane8 & 7) < 4, left, right), v)
            ep[c, 6] = v

    @pl.when(ax < 2)
    def _():
        prepare()

    pl.semaphore_wait(barrier, 2 + jnp.where(me == HUB, NA - 1, jnp.where(me == 0, 0, 1)))
    for c in axial + caxial:
        c.start()

    def tell(d, _):
        pl.semaphore_signal(all_in, inc=1, device_id={"azim": d}, device_id_type=MESH)
        return 0

    lax.fori_loop(0, jnp.where(me == HUB, NA - 1, 0), tell, 0)

    @pl.when(ax >= 2)
    def _():
        prepare()

    def bcast(x):
        return jnp.broadcast_to(x, (8, 128))

    def tap_cells(d):
        cols = pl.ds(pl.multiple_of(d * SEC, SEC), SEC)
        ws = [yw[k : k + 1, cols] for k in range(4)]
        total = ws[0] + ws[1] + ws[2] + ws[3]
        cells = []
        for k in range(4):
            tap = bcast(yt[k : k + 1, cols])
            row = ((tap >> 6) * 43691) >> 17
            cells.append((row - me * ROWS, tap - row * NC, bcast(ws[k] / total)))
        return cells

    def share(d, _):
        acc = [jnp.zeros((8, 128), jnp.float32) for _ in range(5)]
        for lrow, col, w in tap_cells(d):
            inside = jnp.logical_and(lrow >= 0, lrow < ROWS)
            side = jnp.logical_or(col < 4, col >= NC - 4)
            idx = (lrow * 8 + jnp.where(col < 4, col, col - (NC - 8))) & 127
            wk = jnp.where(jnp.logical_and(inside, side), w, 0.0)
            for c in range(5):
                acc[c] = acc[c] + wk * jnp.take_along_axis(ep[c, 6], idx, axis=1)
        for c in range(5):
            shs[d, c] = acc[c]
        return 0

    lax.fori_loop(0, NA, share, 0, unroll=4)

    r0 = jnp.where(me == 0, 0, ROWS - 4)

    @pl.when(jnp.logical_or(me == 0, me == NA - 1))
    def _():
        for c in range(5):
            for r in range(4):
                ep[c, r] = cv[c, r0 + r + 1, :, 0:128]
            for j in range(2):
                even = cv[c, r0 + 2 * j + 1, :, 128:256]
                odd = cv[c, r0 + 2 * j + 2, :, 128:256]
                ep[c, 4 + j] = jnp.where(lane8 < 64, even, pltpu.roll(odd, 64, 1))

    def outer(d, _):
        acc = [shs[d, c] for c in range(5)]
        for lrow, col, w in tap_cells(d):
            r = lrow - r0
            mid = jnp.logical_and(col >= 4, col < NC - 4)
            ok = jnp.logical_and(mid, jnp.logical_and(r >= 0, r < 4))
            wk = jnp.where(ok, w, 0.0)
            high = col >= 128
            group = jnp.where(high, 4 + (r >> 1), r)
            idx = jnp.where(high, (col & 63) + ((r & 1) << 6), col) & 127
            for s in range(6):
                ws = jnp.where(group == s, wk, 0.0)
                for c in range(5):
                    acc[c] = acc[c] + ws * jnp.take_along_axis(ep[c, s], idx, axis=1)
        for c in range(5):
            shs[d, c] = acc[c]
        return 0


    def sh_copy(d):
        return remote(shs.at[d], shr.at[me], sh_s.at[d], sh_r.at[me], {"azim": d})

    def send_share(d, _):
        @pl.when(d != me)
        def _():
            sh_copy(d).start()

        return 0

    even = lax.rem(ax, 2) == 0

    @pl.when(jnp.logical_and(even, me == HUB))
    def _():
        outer(0, 0)

    @pl.when(jnp.logical_and(even, me != 0))
    def _():
        sh_copy(0).start()

    def outer_and_send(d, _):
        outer(d, 0)
        return send_share(d, 0)

    lane_s = lax.broadcasted_iota(jnp.int32, (SEC, 128), 1)
    own = pl.ds(pl.multiple_of(me * SEC, SEC), SEC)
    cosine = jnp.broadcast_to(trig[0:1, own], (8, 128))
    sine = jnp.broadcast_to(trig[1:2, own], (8, 128))

    def trace():
        for c in planes:
            c.wait()
        tt = jnp.zeros((SEC, 128), jnp.float32)
        for p in range(PL):
            for c in range(5):
                ch = c * 8 + p
                x = qv[c, p, :, 0:128]
                tt = jnp.where(lane_s == ch, pltpu.roll(x, ch, 1) if ch else x, tt)
        tt = tt.T
        tq = [tt[8 * c : 8 * c + 8, :] for c in range(5)]
        cart = [tq[0], tq[1], tq[3] * cosine - tq[2] * sine, tq[3] * sine + tq[2] * cosine, tq[4]]
        ends = jnp.zeros((8, 128), jnp.float32)
        for c in range(5):
            trs[c] = cart[c]
            trr[me, c] = cart[c]
            head = pltpu.roll(cart[c], 16 * c, 1) if c else cart[c]
            tail = pltpu.roll(cart[c], (16 * c + 16) % 128, 1)
            ends = jnp.where((lane8 >> 4) == c, jnp.where((lane8 & 15) < 8, head, tail), ends)
        trs[5] = ends

    first, last = lane8 == 0, lane8 == 127
    zero8 = jnp.zeros((8, 128), jnp.float32)
    wide_first = lax.broadcasted_iota(jnp.int32, (W, 128), 1) == 0
    wide_last = lax.broadcasted_iota(jnp.int32, (W, 128), 1) == 127
    for c in range(5):
        for h in range(2):
            m2s[c, h, 2 * W - 8 : 2 * W, :] = zero8
            p2s[c, h, 2 * W + SEC : 2 * W + SEC + 8, :] = zero8
        ov[c, 1, W : W + SEC, :] = jnp.zeros((SEC, NR), jnp.float32)

    def cycle_plane(p, _):
        for b in range(SEC // W + 1):
            rows, prev, now = pl.ds(W * b + W, W), pl.ds(W * b, W), pl.ds(W * b + 2 * W, W)
            if b < SEC // W:
                q = [qv[c, p, W * b : W * b + W, :] for c in range(5)]
                _, f1, f2, f3 = fluxes(q)
                row = lambda k: jnp.broadcast_to(tab[k : k + 1, :], (W, NR))
                ka, ba, cp, cm, cc, so = [row(k) for k in range(6)]
                for c in range(5):
                    ov[c, p, rows, :] += q[c] - f1[c]
                    acc = ov[c, p + 1, rows, :] + cc * q[c]
                    ov[c, p + 2, rows, :] = q[c] + f1[c]
                    base = BR * q[c]
                    p3 = base - cp * f3[c]
                    m3 = base + cm * f3[c]
                    pl0, pl1 = pltpu.roll(p3[:, :128], 127, 1), pltpu.roll(p3[:, 128:], 127, 1)
                    ml0, ml1 = pltpu.roll(m3[:, :128], 1, 1), pltpu.roll(m3[:, 128:], 1, 1)
                    wall = m3[:, 128:] if c != 3 else -m3[:, 128:]
                    lo = jnp.where(wide_last, pl1, pl0) + jnp.where(wide_first, 0.0, ml0)
                    hi = jnp.where(wide_last, wall, pl1) + jnp.where(wide_first, ml0, ml1)
                    acc = acc + jnp.concatenate([lo, hi], axis=1)
                    if c == 2:
                        acc = acc - so * f2[3]
                    if c == 3:
                        acc = acc + so * f2[2]
                    ov[c, p + 1, rows, :] = acc
                    bq, kf = ba * q[c], ka * f2[c]
                    p2, m2 = bq - kf, bq + kf
                    for h in range(2):
                        half = slice(128 * h, 128 * h + 128)
                        p2s[c, h, now, :] = p2[:, half]
                        m2s[c, h, now, :] = m2[:, half]
            if b:
                for c in range(5):
                    for h in range(2):
                        half = slice(128 * h, 128 * h + 128)
                        up = p2s[c, h, pl.ds(W * b + W + 1, W), :]
                        dn = m2s[c, h, pl.ds(W * b + W - 1, W), :]
                        ov[c, p + 1, prev, half] += up + dn
        return 0

    ahead = jnp.where(me == 0, 0, jnp.maximum((12 - me) // 4, 0))
    trace()

    @pl.when(me == 0)
    def _():
        lax.fori_loop(0, NA, outer, 0, unroll=2)

    def tr_copy(d, src, edge):
        if edge:
            return remote(trs.at[5], tre.at[src], tr_s.at[d], tr_r.at[src], {"azim": d})
        return remote(trs.at[0:5], trr.at[src], tr_s.at[d], tr_r.at[src], {"azim": d})

    def is_in(x, items):
        hit = x == items[0]
        for it in items[1:]:
            hit = jnp.logical_or(hit, x == it)
        return hit

    between = jnp.logical_and(me != 0, me != HUB)

    for edge in range(2):

        @pl.when(jnp.logical_and(between, is_in(me, needed(0)[edge])))
        def _(edge=edge):
            tr_copy(0, me, edge).start()

    @pl.when(jnp.logical_and(between, jnp.logical_not(even)))
    def _():
        sh_copy(0).start()

    lax.fori_loop(0, ahead, cycle_plane, 0)

    @pl.when(me != HUB)
    def _():
        pl.semaphore_wait(all_in, 1)

    for a in range(NA):
        for edge in range(2):
            givers = [s for s in needed(a)[edge] if a or s == HUB]
            if givers:

                @pl.when(is_in(me, givers))
                def _(a=a, edge=edge):
                    tr_copy(a, me, edge).start()

    for c in azim:
        c.start()

    @pl.when(me > 0)
    def _():
        crow_dn.start()

    @pl.when(me < NA - 1)
    def _():
        crow_up.start()

    @pl.when(me == NA - 1)
    def _():
        lax.fori_loop(jnp.where(even, 1, 0), NA, outer_and_send, 0)

    @pl.when(me != NA - 1)
    def _():
        lax.fori_loop(1, NA, send_share, 0)

    for c in range(5):
        shr[me, c] = shs[me, c]

    lax.fori_loop(ahead, PL, cycle_plane, 0)

    for s in range(NA):
        for edge in range(2):
            takers = [a for a in range(NA) if s in needed(a)[edge]]
            if takers:

                @pl.when(is_in(me, takers))
                def _(s=s, edge=edge):
                    tr_copy(s, s, edge).wait_recv()
                    if edge:
                        for c in range(5):
                            ends = tre[s]
                            head = pltpu.roll(ends, 128 - 16 * c, 1) if c else ends
                            tail = pltpu.roll(ends, 112 - 16 * c, 1)
                            trr[s, c] = jnp.where(lane8 < 8, head, tail)

    s0 = ((32 * me + 2040) >> 7) & 15
    s1 = ((32 * me + 37) >> 7) & 15

    def ghost(start, shift, sectors):
        vals = [zero8 for _ in range(5)]
        ws = [bcast_roll(cw[k : k + 1, start : start + 256], shift) for k in range(4)]
        total = ws[0] + ws[1] + ws[2] + ws[3]
        for k in range(4):
            tap = bcast_roll(ct[k : k + 1, start : start + 256], shift)
            idx = tap & 127
            sec = tap >> 7
            w = ws[k] / total
            for c in range(5):
                v = jnp.take_along_axis(trr[sectors[0], c], idx, axis=1)
                for s in sectors[1:]:
                    v = jnp.where(sec == s, jnp.take_along_axis(trr[s, c], idx, axis=1), v)
                vals[c] = vals[c] + w * v
        return vals

    def bcast_roll(x, shift):
        full = jnp.broadcast_to(x, (8, 256))
        if isinstance(shift, int):
            return (pltpu.roll(full, 256 - shift, 1) if shift else full)[:, :128]
        return pltpu.roll(full, shift, 1)[:, :128]

    def col_terms(g):
        return fluxes(g)[3]

    back = lax.rem(512 - ROWS * me, 256)
    g = ghost(0, back, [s0, s1])
    f = col_terms(g)
    for c in range(5):
        gl[c] = BC * g[c] + AC * f[c]
    back = lax.rem(512 - 64 - ROWS * me, 256)
    g = ghost(128, back, [(s0 + 4) & 15, (s1 + 4) & 15])
    f = col_terms(g)
    for c in range(5):
        gr[c] = BC * g[c] - AC * f[c]

    @pl.when(me > 0)
    def _():
        crow_up.wait_recv()
        for c in range(5):
            cv[c, 0, :, 0:128] = crlo[c, :, 0:128]
            cv[c, 0, :, 128:192] = crlo[c, :, 128:192]

    @pl.when(me < NA - 1)
    def _():
        crow_dn.wait_recv()
        for c in range(5):
            cv[c, ROWS + 1, :, 0:128] = crhi[c, :, 0:128]
            cv[c, ROWS + 1, :, 128:192] = crhi[c, :, 128:192]

    @pl.when(me == 0)
    def _():
        for h in range(2):
            g = ghost(384, 0, list(range(7, 13))) if h == 0 else ghost(384, 128, list(range(7, 13)))
            for c in range(5):
                cv[c, 0, :, 128 * h : 128 * h + 128] = g[c]

    @pl.when(me == NA - 1)
    def _():
        g = ghost(512, 64, [11, 12, 13, 14, 15, 0])
        for c in range(5):
            cv[c, ROWS + 1, :, 0:128] = g[c]
        g = ghost(512, 192, [11, 12, 13, 14, 15, 0])
        for c in range(5):
            cv[c, ROWS + 1, :, 128:256] = g[c]

    for c in caxial:
        c.wait_recv()

    sub = lax.broadcasted_iota(jnp.int32, (8, 256), 0)
    q = [cv[c, 0, :, :] for c in range(5)]
    f2 = fluxes(q)[2]
    for c in range(5):
        oc[c, 1] = BC * q[c] + AC * f2[c]
    for i in range(1, ROWS + 1):
        q = [cv[c, i, :, :] for c in range(5)]
        _, f1, f2, f3 = fluxes(q)
        x = [chx[c, i - 1, :, :] for c in range(5)]
        x = [jnp.concatenate([v, jnp.ones((8, 64), jnp.float32)], axis=1) for v in x]
        xf = fluxes(x)[1]
        for c in range(5):
            m1 = pltpu.roll(q[c] + f1[c], 1, 0)
            p1 = pltpu.roll(q[c] - f1[c], 7, 0)
            m1 = jnp.where(sub == 0, x[c] + xf[c], m1)
            p1 = jnp.where(sub == 7, x[c] - xf[c], p1)
            acc = oc[c, i] + CC * q[c] + m1 + p1
            base = BC * q[c]
            p3, m3 = base - AC * f3[c], base + AC * f3[c]
            a, bb = pltpu.roll(p3[:, :128], 127, 1), pltpu.roll(p3[:, 128:], 127, 1)
            e, f = pltpu.roll(m3[:, :128], 1, 1), pltpu.roll(m3[:, 128:], 1, 1)
            lg = pltpu.roll(gl[c], 129 - i, 1) if i > 1 else gl[c]
            rg = pltpu.roll(gr[c], 64 - i, 1)
            lo = jnp.where(last, bb, a) + jnp.where(first, lg, e)
            hi = jnp.where(lane8 == 63, rg, bb) + jnp.where(first, e, f)
            acc = acc + jnp.concatenate([lo, hi], axis=1)
            p2, m2 = base - AC * f2[c], base + AC * f2[c]
            if i > 1:
                done = BX * (oc[c, i - 1] + p2)
                cres[c, i - 2, :, 0:128] = done[:, 0:128]
                cres[c, i - 2, :, 128:192] = done[:, 128:192]
            oc[c, i] = acc
            if i < ROWS:
                oc[c, i + 1] = m2
    q = [cv[c, ROWS + 1, :, :] for c in range(5)]
    f2 = fluxes(q)[2]
    for c in range(5):
        done = BX * (oc[c, ROWS] + BC * q[c] - AC * f2[c])
        cres[c, ROWS - 1, :, 0:128] = done[:, 0:128]
        cres[c, ROWS - 1, :, 128:192] = done[:, 128:192]

    def await_share(d, _):
        @pl.when(d != me)
        def _():
            remote(shs.at[d], shr.at[d], sh_s.at[d], sh_r.at[d], {"azim": d}).wait_recv()

        return 0

    lax.fori_loop(0, NA, await_share, 0)
    cart = [functools.reduce(jnp.add, [shr[d, c] for d in range(NA)]) for c in range(5)]
    g = [cart[0], cart[1], cart[3] * cosine - cart[2] * sine, cart[2] * cosine + cart[3] * sine, cart[4]]
    f3 = fluxes(g)[3]
    for c in range(5):
        xm[8 * c : 8 * c + 8, :] = BR * g[c] + INNER * f3[c]
    fix[...] = xm[...].T
    for c in azim + axial:
        c.wait_recv()

    for c in axial + azim + caxial:
        c.wait_send()

    @pl.when(me > 0)
    def _():
        crow_dn.wait_send()

    @pl.when(me < NA - 1)
    def _():
        crow_up.wait_send()

    for a in range(NA):
        for edge in range(2):
            givers = needed(a)[edge]
            if givers:

                @pl.when(is_in(me, givers))
                def _(a=a, edge=edge):
                    tr_copy(a, me, edge).wait_send()

    def drain(d, _):
        @pl.when(d != me)
        def _():
            sh_copy(d).wait_send()

        return 0

    lax.fori_loop(0, NA, drain, 0)


def closing(ov, hal, ah, fix, core, tab, cyc_out, cor_out, buf, sems):
    core_copy = pltpu.make_async_copy(core, cor_out, sems.at[PL])
    core_copy.start()
    top = lax.broadcasted_iota(jnp.int32, (8, NR), 0) == 0
    bottom = lax.broadcasted_iota(jnp.int32, (8, NR), 0) == 7
    first = lax.broadcasted_iota(jnp.int32, (W, 128), 1) == 0
    ka = jnp.broadcast_to(tab[0:1, :], (8, NR))
    ba = jnp.broadcast_to(tab[1:2, :], (8, NR))

    def copy(p):
        return pltpu.make_async_copy(buf.at[:, p], cyc_out.at[:, p], sems.at[p])

    def plane(p, axial):
        side = [ah[c, p, :, :] for c in range(5)]
        f2 = fluxes(side)[2]
        lo = [jnp.where(top, ba * side[c] + ka * f2[c], 0.0) for c in range(5)]
        hi = [jnp.where(bottom, ba * side[c] - ka * f2[c], 0.0) for c in range(5)]
        for b in range(SEC // W):
            rows = slice(W * b, W * b + W)
            if axial is not None:
                q = [hal[c, axial, rows, :] for c in range(5)]
                f1 = fluxes(q)[1]
            inner = fix[rows, :]
            for c in range(5):
                v = ov[c, p + 1, W * b + W : W * b + 2 * W, :]
                if axial == 0:
                    v = v + (q[c] + f1[c])
                if axial == 1:
                    v = v + (q[c] - f1[c])
                if b == 0:
                    v = jnp.concatenate([v[:8] + lo[c], v[8:]], axis=0)
                if b == SEC // W - 1:
                    v = jnp.concatenate([v[: W - 8], v[W - 8 :] + hi[c]], axis=0)
                col = jnp.where(first, pltpu.roll(inner, lax.rem(128 - 8 * c - p, 128), 1), 0.0)
                buf[c, p, rows, 0:128] = BX * (v[:, :128] + col)
                buf[c, p, rows, 128:256] = BX * v[:, 128:]
        copy(p).start()

    def middle(p, _):
        plane(p, None)
        return 0

    lax.fori_loop(1, PL - 1, middle, 0)
    plane(jnp.int32(0), 0)
    plane(jnp.int32(PL - 1), 1)
    core_copy.wait()
    for p in range(PL):
        copy(p).wait()


def body(cycle_state, core_state, core_taps, core_weights, cycle_taps, cycle_weights):
    tab, trig = tables()
    f32, i32 = jnp.float32, jnp.int32
    dma = pltpu.SemaphoreType.DMA
    core_t = jnp.transpose(core_state, (0, 2, 1, 3))
    hbm = pl.BlockSpec(memory_space=pltpu.HBM)
    vmem = pl.BlockSpec(memory_space=pltpu.VMEM)
    vm = pltpu.VMEM
    shape = lambda *dims: jax.ShapeDtypeStruct(dims, f32)
    operands = [
        pltpu.with_memory_space_constraint(x, pltpu.HBM)
        for x in (
            cycle_state, core_t, core_taps.T, core_weights.T, cycle_taps.T, cycle_weights.T,
            jnp.asarray(tab), jnp.asarray(trig),
        )
    ]
    parts = pl.pallas_call(
        kernel,
        out_shape=(
            shape(5, PL + 2, SEC + W, NR),
            shape(5, 2, SEC, NR),
            shape(5, PL, 8, NR),
            shape(128, 128),
            shape(5, ROWS, PL, NC),
            shape(8, NR),
        ),
        in_specs=[hbm] * 8,
        out_specs=(vmem,) * 6,
        scratch_shapes=[
            vm((5, PL, SEC, NR), f32),
            vm((5, 2, SEC + 4 * W, 128), f32),
            vm((5, 2, SEC + 4 * W, 128), f32),
            vm((5, ROWS, PL, NC), f32),
            vm((5, ROWS + 2, PL, 256), f32),
            vm((5, ROWS + 2, PL, 256), f32),
            vm((5, ROWS, PL, NC), f32),
            vm((5, PL, NC), f32),
            vm((5, PL, NC), f32),
            vm((6, 8, 128), f32),
            vm((NA, 8, 128), f32),
            vm((NA, 5, 8, 128), f32),
            vm((NA, 5, 8, 128), f32),
            vm((NA, 5, 8, 128), f32),
            vm((128, 128), f32),
            vm((5, 7, 8, 128), f32),
            vm((5, 8, 128), f32),
            vm((5, 8, 128), f32),
            vm((8, NT), f32),
            vm((4, 768), i32),
            vm((4, 768), f32),
            vm((4, NT), i32),
            vm((4, NT), f32),
            pltpu.SemaphoreType.REGULAR,
            dma((PL,)),
            dma((7,)),
            dma((2,)), dma((2,)), dma((2,)), dma((2,)), dma((2,)), dma((2,)), dma((2,)), dma((2,)),
            dma((NA,)), dma((NA,)), dma((NA,)), dma((NA,)),
        ],
        compiler_params=pltpu.CompilerParams(
            collective_id=0, has_side_effects=True, vmem_limit_bytes=24 * 2**20
        ),
    )(*operands)
    cycle_new, core_new = pl.pallas_call(
        closing,
        out_shape=(
            jax.ShapeDtypeStruct(cycle_state.shape, f32),
            jax.ShapeDtypeStruct(core_t.shape, f32),
        ),
        in_specs=[vmem] * 6,
        out_specs=(hbm, hbm),
        scratch_shapes=[vm((5, PL, SEC, NR), f32), dma((PL + 1,))],
        compiler_params=pltpu.CompilerParams(vmem_limit_bytes=12 * 2**20),
    )(*parts)
    return cycle_new, jnp.transpose(core_new, (0, 2, 1, 3))


def solution(mesh):
    placed = (P(None, "axial", "azim", None), P(None, "axial", "azim", None), P(), P(), P(), P())
    return jax.shard_map(
        body,
        mesh=mesh,
        in_specs=placed,
        out_specs=(P(None, "axial", "azim", None), P(None, "axial", "azim", None)),
        check_vma=False,
    )
```
